32 devices in a mesh: groups: 2 (over x), win: 16 (over z, y, core).
Axes of the slice: x: 2, y: 2, z: 4, core: 2. Of those that a mesh axis runs over, the one named last changes fastest.
Arguments:
- latents: bfloat16 [6, 8, 256, 1536], P('groups', None, 'win'), parts along dimension 0, may hold values from -60 to 60
- offsets: int32 [6], P('groups'), parts along dimension 0, may hold values from 0 to 8, as said below
- levels: int32 [6], P('groups'), parts along dimension 0, may hold values from 0 to 31
- mod_table: bfloat16 [32, 6, 1536], replicated, may hold values from -3 to 3
- rel_bias: float32 [6, 64, 64], replicated, may hold values from -3 to 403
- w_qkv: bfloat16 [1536, 2304], P('win'), may hold values from -0.15625 to 0.15625
- w_out: bfloat16 [768, 1536], P('win'), may hold values from -0.21875 to 0.21875
- w_up: bfloat16 [1536, 3072], P('win'), may hold values from -0.15625 to 0.15625
- w_down: bfloat16 [3072, 1536], P('win'), may hold values from -0.109375 to 0.109375
Outputs:
- result: bfloat16 [6, 8, 256, 1536], P('groups', None, 'win'), parts along dimension 0
The draws below stay inside these ranges and needn't reach their ends.
There are 2 independent parts, one for each index of `groups`. The reference program is written for one: setup_inputs(seed, part) draws one part's arguments, and reference() takes and returns one part's arrays. A program takes and returns all parts, laid end to end along the dimension named above; an argument that names none is the same for every part. Nothing has to cross between parts.
Inputs may be any that keep to these rules, and one draw needn't show every extreme that they name: `offsets`: some micro-batch has offset 8 in every draw.
All inputs are finite; a program needn't handle non-finite values.
Results may differ from the reference program's by a relative error of at most 0.007.
Values may be sent and summed in bfloat16 or wider, within the bound.
A program may use at most 128 MiB of HBM per device.

```python
import jax
import jax.numpy as jnp
from jax import lax

D = 1536
HEADS = 6
HEAD_DIM = 128
FF = 3072
WIN = 8
LEVELS = 32
MB = 3
LON = 256


def draw_latents(key, part):
    first = jax.random.fold_in(jax.random.fold_in(key, 11), 0)
    base = jax.random.normal(first, (MB, WIN, LON, D), jnp.float32)
    return jnp.clip(base, -6.0, 6.0).astype(jnp.bfloat16)


def draw_rel_bias(key, part):
    keys = jax.random.split(jax.random.fold_in(key, 23), 1)
    width = WIN * WIN
    base = jnp.clip(jax.random.normal(keys[0], (HEADS, width, width), jnp.float32), -3.0, 3.0)
    return base.astype(jnp.float32)


def draw_offsets(key, part):
    first, second = jax.random.split(jax.random.fold_in(key, 37))
    values_drawn = jax.random.randint(first, (MB,), 0, WIN + 1)
    place = jax.random.randint(second, (), 0, MB)
    return jnp.where(jnp.arange(MB, dtype=jnp.int32) == place, WIN, values_drawn).astype(jnp.int32)


def block_levels(key, dims, shards, least, top_value):
    def one(dim, blocks):
        draws = jax.random.uniform(jax.random.fold_in(jax.random.fold_in(key, 6), dim), (blocks,), jnp.float32, least / len(shards), top_value / len(shards))
        return jnp.repeat(jnp.exp(draws), dims[dim] // blocks).reshape((-1,) + (1,) * (len(dims) - dim - 1))

    level = one(*shards[0])
    for cut in shards[1:]:
        level = level * one(*cut)
    return level


def bell_draw(key, extent, scale, most, shards=(), kind=jnp.bfloat16):
    factor_of = block_levels(key, extent, shards, -0.22, 0.18) if shards else 1.0
    drawn = jax.random.normal(key, extent, jnp.float32) * scale * factor_of
    return jnp.minimum(jnp.maximum(drawn, -most), most).astype(kind)


def setup_inputs(seed: int = 0, part: int = 0) -> dict:
    splits = jax.random.split(jax.random.key(seed), 10)
    part_splits = jax.random.split(jax.random.fold_in(splits[9], part), 10)
    return {
        "latents": draw_latents(jax.random.fold_in(jax.random.fold_in(splits[9], part), 71), part),
        "offsets": draw_offsets(jax.random.fold_in(jax.random.fold_in(splits[9], part), 71), part),
        "levels": jax.random.randint(part_splits[2], (MB,), 0, LEVELS).astype(jnp.int32),
        "mod_table": bell_draw(splits[3], (LEVELS, 6, D), 0.5, 3.0),
        "rel_bias": draw_rel_bias(jax.random.fold_in(splits[9], 71), part),
        "w_qkv": bell_draw(splits[5], (D, 3 * HEADS * HEAD_DIM), D ** -0.5, 0.15625, ((0, 16),)),
        "w_out": bell_draw(splits[6], (HEADS * HEAD_DIM, D), (HEADS * HEAD_DIM) ** -0.5, 0.21875, ((0, 16),)),
        "w_up": bell_draw(splits[7], (D, FF), D ** -0.5, 0.15625, ((0, 16),)),
        "w_down": bell_draw(splits[8], (FF, D), FF ** -0.5, 0.109375, ((0, 16),)),
    }


def norm_rows(values_in):
    centre = values_in - lax.optimization_barrier(jnp.mean(values_in, axis=-1, keepdims=True))
    spread = lax.optimization_barrier(jnp.mean(centre * centre, axis=-1, keepdims=True))
    return centre * lax.rsqrt(spread + 1e-06)

def reference(latents, offsets, levels, mod_table, rel_bias, w_qkv, w_out, w_up, w_down):
    batches, lat_rows, columns, features = latents.shape
    inner = HEADS * HEAD_DIM
    selector = (levels[:, None] == jnp.arange(LEVELS, dtype=jnp.int32)[None, :]).astype(jnp.float32)
    modulation = jnp.einsum('ml,lkd->mkd', selector, mod_table.astype(jnp.float32))
    modulation = modulation.reshape(batches, 6, 1, 1, features)
    stream = latents.astype(jnp.float32)
    normed = (norm_rows(stream) * (1.0 + modulation[:, 0]) + modulation[:, 1]).astype(jnp.bfloat16)
    rolled = jax.vmap(lambda region, shift_by: jnp.roll(region, shift_by, axis=1))(normed, offsets)
    per_row = columns // WIN
    windows = rolled.reshape(batches, lat_rows, per_row, WIN, features).transpose(0, 2, 1, 3, 4)
    windows = windows.reshape(-1, lat_rows * WIN, features)
    number = windows.shape[0]
    triple = jnp.dot(windows.reshape(-1, features), w_qkv, preferred_element_type=jnp.float32)
    triple = triple.astype(jnp.bfloat16).reshape(number, lat_rows * WIN, 3, HEADS, HEAD_DIM)
    triple = triple.astype(jnp.float32)
    scores = jnp.einsum('wqhe,wkhe->whqk', triple[:, :, 0], triple[:, :, 1]) * (1.0 / HEAD_DIM ** 0.5)
    scores = scores + rel_bias[None]
    probs = jax.nn.softmax(scores, axis=-1).astype(jnp.bfloat16)
    attended = jnp.einsum('whqk,wkhe->wqhe', probs.astype(jnp.float32), triple[:, :, 2]).astype(jnp.bfloat16)
    projected = jnp.dot(attended.reshape(-1, inner), w_out, preferred_element_type=jnp.float32)
    projected = projected.reshape(batches, per_row, lat_rows, WIN, features).transpose(0, 2, 1, 3, 4)
    projected = projected.reshape(batches, lat_rows, columns, features)
    projected = jax.vmap(lambda region, shift_by: jnp.roll(region, -shift_by, axis=1))(projected, offsets)
    middle = (stream + modulation[:, 2] * projected).astype(jnp.bfloat16)
    second = (norm_rows(middle.astype(jnp.float32)) * (1.0 + modulation[:, 3]) + modulation[:, 4]).astype(jnp.bfloat16)
    hidden = jnp.dot(second.reshape(-1, features), w_up, preferred_element_type=jnp.float32)
    hidden = jax.nn.gelu(hidden, approximate=False).astype(jnp.bfloat16)
    lowered = jnp.dot(hidden, w_down, preferred_element_type=jnp.float32).reshape(batches, lat_rows, columns, features)
    return (middle.astype(jnp.float32) + modulation[:, 5] * lowered).astype(jnp.bfloat16)
```

```python
import functools

import jax
import jax.numpy as jnp
from jax import lax
from jax.experimental import pallas as pl
from jax.experimental.pallas import tpu as pltpu
from jax.sharding import PartitionSpec as P

HEADS = 6
HEAD_DIM = 128
WIN = 8
LEVELS = 32

MESH = pl.DeviceIdType.MESH
LINE = 4
LAT, STRIP, ATT, PART = 0, 3, 15, 18
UP_CHUNKS = 2
DOWN_CHUNKS = 4


def under(condition, act):
    if condition is None:
        act()
    else:
        pl.when(condition)(act)


def both(one, other):
    return other if one is None else one & other


class Chunk:
    def __init__(self, full, depth, rows_by_y, first, width, by_rows, base):
        self.full, self.depth, self.rows_by_y = full, depth, rows_by_y
        self.first, self.width, self.by_rows, self.base = first, width, by_rows, base
        self.kinds = 2 if rows_by_y else 1
        self.count = 1 + 3 * LINE * self.kinds + 2 * LINE * self.kinds

    def region(self, z, y, c, h=None):
        at = (z * 2 + y) * 2 + c if self.rows_by_y else z * 2 + c
        start, size = at * self.depth, self.depth
        first, width = self.first, self.width
        if h is not None and self.by_rows:
            size = self.depth // 2
            start = start + h * size
        elif h is not None:
            width = self.width // 2
            first = pl.multiple_of(self.first + h * width, 128)
        return self.full.at[pl.ds(pl.multiple_of(start, 16), size), pl.ds(first, width)]

    def slot(self, kind, z, k=0):
        return self.base + 1 + kind * LINE * self.kinds + z * self.kinds + k

    def hand_slot(self, z, k, h):
        return self.base + 1 + 3 * LINE * self.kinds + (z * self.kinds + k) * 2 + h


UPWARD, DOWNWARD, ACROSS = 0, 1, 2


class Gather:
    def __init__(self, send, recv):
        self.send, self.recv = send, recv
        me = lax.axis_index("win")
        self.c = lax.rem(me, 2)
        self.y = lax.rem(me // 2, 2)
        self.z = me // 4
        self.g = lax.axis_index("groups")
        self.x = lax.rem(self.g, 2)
        up, down = lax.rem(self.z + 1, LINE), lax.rem(self.z + LINE - 1, LINE)
        self.to_up = {"win": self.place(up, self.y, self.c)}
        self.to_down = {"win": self.place(down, self.y, self.c)}
        self.to_y = {"win": self.place(self.z, 1 - self.y, self.c)}
        self.to_core = {"win": self.place(self.z, self.y, 1 - self.c)}
        self.to_x = {"groups": self.g + 1 - 2 * self.x}
        far = lax.rem(self.z + 2 * self.c + LINE - 1, LINE)
        self.to_far = {"win": self.place(far, self.y, 1 - self.c)}
        self.started = []

    def place(self, z, y, c):
        return (z * 2 + y) * 2 + c

    def neighbours(self):
        return [self.to_up, self.to_down, self.to_y, self.to_core, self.to_x, self.to_far]

    def copy(self, slot, src, dst, to):
        return pltpu.make_async_remote_copy(
            src_ref=src,
            dst_ref=dst,
            send_sem=self.send.at[slot],
            recv_sem=self.recv.at[slot],
            device_id=to,
            device_id_type=MESH,
        )

    def put(self, condition, make):
        under(condition, lambda: make().start())
        self.started.append((condition, make))

    def pass_on(self, condition, slot, part, to):
        self.put(condition, lambda: self.copy(slot, part(), part(), to))

    def arrive(self, condition, slot, part):
        under(condition, lambda: self.copy(slot, part(), part(), self.to_core).wait_recv())

    def side(self, k):
        return self.y if k == 0 else 1 - self.y

    def piece(self, t, z, k, h=None, c=None):
        return lambda: t.region(z, self.side(k), self.c if c is None else c, h)

    def y_send(self, t, source):
        self.put(None, lambda: self.copy(t.base, source(), self.piece(t, self.z, 0, self.x)(), self.to_y))

    def own(self, t):
        part = self.piece(t, self.z, 0, self.x)
        self.pass_on(self.z >= 1, t.slot(DOWNWARD, self.z), part, self.to_down)
        self.pass_on(self.z + 1 < LINE, t.slot(UPWARD, self.z), part, self.to_up)
        self.pass_on(None, t.hand_slot(self.z, 0, 0), self.piece(t, self.z, 0), self.to_core)

    def y_come(self, t):
        part = self.piece(t, self.z, 1, self.x)
        self.arrive(None, t.base, part)
        self.pass_on(self.z >= 1, t.slot(DOWNWARD, self.z, 1), part, self.to_down)
        self.pass_on(self.z + 1 < LINE, t.slot(UPWARD, self.z, 1), part, self.to_up)
        self.pass_on(None, t.slot(ACROSS, self.z, 1), part, self.to_x)
        self.pass_on(None, t.hand_slot(self.z, 1, self.x), part, self.to_core)

    def sources(self, d):
        if d == 0:
            return ((None, self.z),)
        return ((self.z >= d, self.z - d), (self.z + d < LINE, self.z + d))

    def z_come(self, t, d):
        ways = ((UPWARD, self.z + 1 < LINE, self.to_up), (DOWNWARD, self.z >= 1, self.to_down))
        for (there, z), (way, more, to) in zip(self.sources(d), ways):
            for k in range(t.kinds):
                part = self.piece(t, z, k, self.x)
                self.arrive(there, t.slot(way, z, k), part)
                if d < LINE - 1:
                    self.pass_on(there & more, t.slot(way, z, k), part, to)
                self.pass_on(there, t.slot(ACROSS, z, k), part, self.to_x)
                self.pass_on(there, t.hand_slot(z, k, self.x), part, self.to_core)

    def x_come(self, t, d):
        for there, z in self.sources(d):
            for k in range(1 if d == 0 else 0, t.kinds):
                part = self.piece(t, z, k, 1 - self.x)
                self.arrive(there, t.slot(ACROSS, z, k), part)
                self.pass_on(there, t.hand_slot(z, k, 1 - self.x), part, self.to_core)

    def handed(self, t):
        other = 1 - self.c
        self.arrive(None, t.hand_slot(self.z, 0, 0), self.piece(t, self.z, 0, None, other))
        for d in range(LINE):
            for there, z in self.sources(d):
                for k in range(1 if d == 0 else 0, t.kinds):
                    for h in range(2):
                        self.arrive(there, t.hand_slot(z, k, h), self.piece(t, z, k, h, other))

    def drain(self):
        for condition, make in self.started:
            under(condition, lambda make=make: make().wait_send())


def meet(neighbours):
    barrier = pltpu.get_barrier_semaphore()
    for to in neighbours:
        pl.semaphore_signal(barrier, inc=1, device_id=to, device_id_type=MESH)
    pl.semaphore_wait(barrier, len(neighbours))


def norm_rows(values_in):
    centre = values_in - jnp.mean(values_in, axis=-1, keepdims=True)
    spread = jnp.mean(centre * centre, axis=-1, keepdims=True)
    return centre * lax.rsqrt(spread + 1e-06)


def passed_along(shard, axis, by):
    length = lax.axis_size(axis)
    return lax.ppermute(shard, axis, [(i, (i + by) % length) for i in range(length)])


def cut(widened, starts, columns):
    return jnp.stack(
        [
            lax.dynamic_slice_in_dim(widened[m], starts[m], columns, 1)
            for m in range(widened.shape[0])
        ]
    )


def restore_grid(region, arrived, offsets, columns):
    return cut(jnp.concatenate([region, arrived], axis=2), offsets, columns)


def plain(latents, offsets, levels, mod_table, rel_bias, w_qkv, w_out, w_up, w_down):
    batches, lat_rows, columns, features = latents.shape
    inner = HEADS * HEAD_DIM
    per_dev = columns // WIN
    selector = (levels[:, None] == jnp.arange(LEVELS, dtype=jnp.int32)[None, :]).astype(
        jnp.bfloat16
    )
    modulation = jnp.dot(
        selector, mod_table.reshape(LEVELS, 6 * features), preferred_element_type=jnp.float32
    )
    modulation = modulation.reshape(batches, 6, 1, 1, features)
    stream = latents.astype(jnp.float32)
    normed = (norm_rows(stream) * (1.0 + modulation[:, 0]) + modulation[:, 1]).astype(jnp.bfloat16)
    arrived = passed_along(normed[:, :, columns - WIN :, :], "win", 1)
    widened = jnp.concatenate([arrived, normed], axis=2)
    rolled = cut(widened, WIN - offsets, columns)
    full_qkv = lax.all_gather(w_qkv, "win", axis=0, tiled=True)
    windows = rolled.reshape(batches, lat_rows, per_dev, WIN, features).transpose(0, 2, 1, 3, 4)
    windows = windows.reshape(-1, lat_rows * WIN, features)
    number = windows.shape[0]
    triple = jnp.dot(windows.reshape(-1, features), full_qkv, preferred_element_type=jnp.float32)
    triple = triple.astype(jnp.bfloat16).reshape(number, lat_rows * WIN, 3, HEADS, HEAD_DIM)
    scores = jnp.einsum(
        "wqhe,wkhe->whqk", triple[:, :, 0], triple[:, :, 1], preferred_element_type=jnp.float32
    )
    scores = scores * (1.0 / HEAD_DIM**0.5) + rel_bias[None]
    probs = jax.nn.softmax(scores, axis=-1).astype(jnp.bfloat16)
    attended = jnp.einsum(
        "whqk,wkhe->wqhe", probs, triple[:, :, 2], preferred_element_type=jnp.float32
    ).astype(jnp.bfloat16)
    attended = attended.reshape(batches, per_dev, lat_rows, WIN, inner).transpose(0, 2, 1, 3, 4)
    attended = attended.reshape(batches, lat_rows, columns, inner)
    full_out = lax.all_gather(w_out, "win", axis=0, tiled=True)
    returned = passed_along(attended[:, :, :WIN, :], "win", -1)
    restored = restore_grid(attended, returned, offsets, columns)
    projected = jnp.dot(restored.reshape(-1, inner), full_out, preferred_element_type=jnp.float32)
    projected = projected.reshape(batches, lat_rows, columns, features)
    middle = (stream + modulation[:, 2] * projected).astype(jnp.bfloat16)
    second = (
        norm_rows(middle.astype(jnp.float32)) * (1.0 + modulation[:, 3]) + modulation[:, 4]
    ).astype(jnp.bfloat16)
    full_up = lax.all_gather(w_up, "win", axis=0, tiled=True)
    hidden = jnp.dot(second.reshape(-1, features), full_up, preferred_element_type=jnp.float32)
    hidden = jax.nn.gelu(hidden, approximate=False).astype(jnp.bfloat16)
    full_down = lax.all_gather(w_down, "win", axis=0, tiled=True)
    lowered = jnp.dot(hidden, full_down, preferred_element_type=jnp.float32).reshape(
        batches, lat_rows, columns, features
    )
    return (middle.astype(jnp.float32) + modulation[:, 5] * lowered).astype(jnp.bfloat16)


def repeat(count, act):
    lax.fori_loop(0, count, lambda i, _: (act(i), 0)[1], 0)


def chunks_of(shapes, fulls):
    (q, o, u, d), base, made = shapes, 0, []

    def take(full, shape, count, rows_by_y, by_rows):
        nonlocal base
        width = full[1] // count
        for i in range(count):
            ref = None if fulls is None else fulls[full[0]]
            made.append(Chunk(ref, shape[0], rows_by_y, i * width, width, by_rows, base))
            base += made[-1].count

    take((0, q[1] // 2), q, 1, True, True)
    take((1, o[1]), o, 1, True, False)
    take((2, u[1] // 2), u, UP_CHUNKS, True, True)
    take((3, d[1]), d, DOWN_CHUNKS, False, True)
    return made, base


def kernel(
    batches, area, offsets_ref, levels_ref, lat_ref, table_ref, bias_ref, s0, s1, s2, s3, out_ref,
    f0, f1, f2, f3, a0, a2, mod, gather_in, gather_out, lat, wide, wins, triple, heads, att, middle,
    second, hidden, part_out, part_in, part_own, send, recv, act_send, act_recv,
):
    features = lat_ref.shape[1]
    own = lat_ref.shape[0] // batches
    moved = gather_in.shape[1]
    inner = f0.shape[1] // 3
    pair_heads = inner // HEAD_DIM
    bf, f32 = jnp.bfloat16, jnp.float32
    chunks, _ = chunks_of((s0.shape, s1.shape, s2.shape, s3.shape), (f0, f1, f2, f3))
    cq, co, cu, cd = chunks[0], chunks[1], chunks[2 : 2 + UP_CHUNKS], chunks[2 + UP_CHUNKS :]
    net = Gather(send, recv)
    x, y, z, c = net.x, net.y, net.z, net.c
    other = 1 - y

    def activation(send_at, recv_at, src, dst, to):
        def make():
            return pltpu.make_async_remote_copy(
                src_ref=src(),
                dst_ref=dst(),
                send_sem=act_send.at[send_at],
                recv_sem=act_recv.at[recv_at],
                device_id=to,
                device_id_type=MESH,
            )

        net.put(None, make)

    def landed(recv_at, dst):
        pltpu.make_async_remote_copy(
            src_ref=dst,
            dst_ref=dst,
            send_sem=act_send.at[recv_at],
            recv_sem=act_recv.at[recv_at],
            device_id=net.to_core,
            device_id_type=MESH,
        ).wait_recv()

    def lay_qkv():
        for which in range(3):
            for k in range(2):
                first = (which * 2 + k) * inner
                a0[k, :, which * inner : (which + 1) * inner] = s0[:, first : first + inner]
        mine = net.place(z, y, c) * s0.shape[0]
        f0[pl.ds(pl.multiple_of(mine, 16), s0.shape[0]), :] = a0[y]

    def lay_out():
        mine = net.place(z, y, c) * s1.shape[0]
        f1[pl.ds(pl.multiple_of(mine, 16), s1.shape[0]), :] = s1[...]

    block = s3.shape[0] * 2

    def lay_up():
        for at in range(LINE):
            for k in range(2):
                first = (at * 2 + k) * block
                a2[k, :, at * block : (at + 1) * block] = s2[:, first : first + block]
        mine = net.place(z, y, c) * s2.shape[0]
        f2[pl.ds(pl.multiple_of(mine, 16), s2.shape[0]), :] = a2[y]

    def lay_down():
        mine = (z * 2 + c) * s3.shape[0]
        f3[pl.ds(pl.multiple_of(mine, 16), s3.shape[0]), :] = s3[...]

    def half_rows(ref, t):
        size = t.depth // 2
        rows = pl.ds(pl.multiple_of(x * size, 16), size)
        return lambda: ref.at[other, rows, pl.ds(t.first, t.width)]

    def send_lat(m):
        activation(
            LAT + m, LAT + m, lambda: lat_ref.at[pl.ds(m * own, own)], lambda: lat.at[y, m], net.to_y
        )

    def modulate():
        for m in range(batches):
            mod[m] = table_ref[levels_ref[m]].astype(f32)

    def make_moves():
        i = lax.broadcasted_iota(jnp.int32, (moved, wide.shape[2]), 0)
        j = lax.broadcasted_iota(jnp.int32, (moved, wide.shape[2]), 1)
        to_row, to_at = (i >> 3) & 7, ((i >> 6) << 3) + (i & 7)
        from_row, from_at = (j >> 3) & 7, ((j >> 6) << 3) + (j & 7)
        same = to_row == from_row
        k = lax.broadcasted_iota(jnp.int32, (own, moved), 0)
        n = lax.broadcasted_iota(jnp.int32, (own, moved), 1)
        back = (k >> 4) == ((n >> 3) & 7)
        back_at, rolled_at = k & 15, ((n >> 6) << 3) + (n & 7)
        for m in range(batches):
            by = offsets_ref[m]
            hit = same & (to_at + WIN - by == from_at)
            gather_in[m] = jnp.where(hit, 1.0, 0.0).astype(bf)
            hit = back & (back_at + by == rolled_at)
            gather_out[m] = jnp.where(hit, 1.0, 0.0).astype(bf)

    def copy_own():
        for m in range(batches):
            lat[y, m] = lat_ref[m * own : (m + 1) * own, :]

    def norm_tile(m, slot):
        def step(i):
            rows = lat[slot, m, pl.ds(pl.multiple_of(i * 32, 32), 32), :].astype(f32)
            value = norm_rows(rows) * (1.0 + mod[m, 0:1, :]) + mod[m, 1:2, :]
            value = value.reshape(2, 2, WIN, features)
            for half in range(2):
                start = pl.multiple_of((half + 1) * area + i * 16, 16)
                wide[m, slot, pl.ds(start, 16), :] = value[:, half].reshape(16, features).astype(bf)

        repeat(own // 32, step)

    def strip(m, slot, at):
        return wide.at[m, slot, pl.ds(at * area, area)]

    def send_strips(m, slot):
        base = STRIP + m * 4
        low_slot = (1 - c) * (1 - slot) + c * slot
        low_z = lax.rem(z + LINE - (1 - c) * (1 - slot), LINE)
        activation(
            base + slot * 2, base + low_slot * 2 + 1,
            lambda: strip(m, slot, 1), lambda: strip(m, low_slot, 3),
            {"win": net.place(low_z, y, 1 - c)},
        )
        high_slot = (1 - c) * slot + c * (1 - slot)
        high_z = lax.rem(z + c * slot, LINE)
        activation(
            base + slot * 2 + 1, base + high_slot * 2,
            lambda: strip(m, slot, 2), lambda: strip(m, high_slot, 0),
            {"win": net.place(high_z, y, 1 - c)},
        )

    def norm_own(m):
        norm_tile(m, y)
        send_strips(m, y)

    def norm_other(m):
        landed(LAT + m, lat.at[other, m])
        norm_tile(m, other)
        send_strips(m, other)

    def windows(m):
        for slot in range(2):
            landed(STRIP + m * 4 + slot * 2, strip(m, slot, 0))
            landed(STRIP + m * 4 + slot * 2 + 1, strip(m, slot, 3))
        for slot in range(2):
            wins[m, slot * moved : (slot + 1) * moved, :] = jnp.dot(
                gather_in[m], wide[m, slot], preferred_element_type=f32
            ).astype(bf)

        def project(i):
            cols = pl.ds(pl.multiple_of(i * inner, 128), inner)
            triple[m, :, cols] = jnp.dot(
                wins[m], f0[:, cols], preferred_element_type=f32
            ).astype(bf)

        repeat(3, project)

    def attend(m):
        def window(w):
            rows = pl.ds(pl.multiple_of(w * area, area), area)
            for head in range(pair_heads):
                def of(which):
                    return triple[m, rows, pl.ds(which * inner + head * HEAD_DIM, HEAD_DIM)]

                scores = lax.dot_general(
                    of(0), of(1), (((1,), (1,)), ((), ())), preferred_element_type=f32
                )
                scores = scores * (1.0 / HEAD_DIM**0.5) + bias_ref[y * pair_heads + head]
                powers = jnp.exp(scores - jnp.max(scores, axis=-1, keepdims=True))
                probs = (powers / jnp.sum(powers, axis=-1, keepdims=True)).astype(bf)
                heads[m, rows, pl.ds(head * HEAD_DIM, HEAD_DIM)] = jnp.dot(
                    probs, of(2), preferred_element_type=f32
                ).astype(bf)

        repeat(2 * moved // area, window)
        mine = pl.ds(pl.multiple_of(y * inner, 128), inner)
        for slot in range(2):
            att[m, pl.ds(slot * own, own), mine] = jnp.dot(
                gather_out[m], heads[m, slot * moved : (slot + 1) * moved, :],
                preferred_element_type=f32,
            ).astype(bf)
        activation(
            ATT + m, ATT + m, lambda: att.at[m, :, mine], lambda: att.at[m, :, mine], net.to_y
        )

    width = 256

    def columns(i):
        return pl.ds(pl.multiple_of(i * width, width), width)

    def settle(m):
        theirs = pl.ds(pl.multiple_of(other * inner, 128), inner)
        landed(ATT + m, att.at[m, :, theirs])

        def piece(i):
            cols = columns(i)
            found = jnp.dot(att[m], f1[:, cols], preferred_element_type=f32)
            for slot in range(2):
                change = mod[m, 2:3, cols] * found[slot * own : (slot + 1) * own]
                middle[slot, m, :, cols] = (lat[slot, m, :, cols].astype(f32) + change).astype(bf)

        repeat(features // width, piece)
        for slot in range(2):
            def again(i):
                start = pl.multiple_of(i * 32, 32)
                rows = middle[slot, m, pl.ds(start, 32), :].astype(f32)
                value = norm_rows(rows) * (1.0 + mod[m, 3:4, :]) + mod[m, 4:5, :]
                second[slot, pl.ds(m * own + start, 32), :] = value.astype(bf)

            repeat(own // 32, again)

    def lift(first, count):
        def piece(i):
            cols = columns(first + i)
            for slot in range(2):
                found = jnp.dot(second[slot], f2[:, cols], preferred_element_type=f32)
                found = 0.5 * found * (1.0 + lax.erf(found * (0.5**0.5)))
                hidden[slot, :, cols] = found.astype(bf)

        repeat(count, piece)

    def lower(j):
        cols = slice(cd[j].first, cd[j].first + cd[j].width)
        part_out[:, cols] = jnp.dot(
            hidden[other], f3[:, cols], preferred_element_type=f32
        ).astype(bf)
        activation(
            PART + j, PART + j, lambda: part_out.at[:, cols], lambda: part_in.at[:, cols], net.to_y
        )
        part_own[:, cols] = jnp.dot(hidden[y], f3[:, cols], preferred_element_type=f32)

    def finish(j):
        cols = slice(cd[j].first, cd[j].first + cd[j].width)
        landed(PART + j, part_in.at[:, cols])
        for m in range(batches):
            rows = slice(m * own, (m + 1) * own)
            change = part_own[rows, cols] + part_in[rows, cols].astype(f32)
            out_ref[rows, cols] = (
                middle[y, m, :, cols].astype(f32) + mod[m, 5:6, cols] * change
            ).astype(bf)

    steps = []

    def at(time, act, *args):
        steps.append((time, len(steps), functools.partial(act, *args)))

    def weight(t, own_at, y_at, zs):
        at(own_at, net.own, t)
        if t.kinds == 2:
            at(y_at, net.y_come, t)
            at(y_at + 1.9, net.x_come, t, 0)
        for d, when in enumerate(zs):
            at(when, net.z_come, t, d + 1)
            at(when + 1.9, net.x_come, t, d + 1)

    at(0, lay_qkv)
    at(0, net.y_send, cq, half_rows(a0, cq))
    at(0.4, send_lat, 0)
    at(0.5, lay_out)
    at(0.5, net.y_send, co, net.piece(co, z, 0, x))
    at(0.6, send_lat, 1)
    at(0.6, send_lat, 2)
    at(0.7, lay_up)
    for t in cu:
        at(0.7, net.y_send, t, half_rows(a2, t))
    at(0.8, lay_down)
    at(0.9, copy_own)
    at(1, modulate)
    for m in range(batches):
        at(1 + 0.1 * m, norm_own, m)
    at(3.8, make_moves)
    weight(cq, 0.1, 4, (7, 13, 19))
    weight(co, 13.1, 17, (27, 31, 36))
    weight(cu[0], 31.1, 39.5, (40, 44, 48))
    weight(cu[1], 44.1, 46, (52, 56, 60))
    last = 56.1
    for j, t in enumerate(cd):
        weight(t, last, None, (63 + 6 * j, 65 + 6 * j, 67 + 6 * j))
        last = 65.1 + 6 * j
    for m, when in enumerate((15, 25, 36.1)):
        at(when, norm_other, m)
    at(22.9, net.handed, cq)
    for m, when in enumerate((23, 30, 43)):
        at(when, windows, m)
        at(when + 0.1, attend, m)
    at(41.9, net.handed, co)
    for m, when in enumerate((42, 46, 56)):
        at(when, settle, m)
    each = f2.shape[1] // width // UP_CHUNKS
    for i, (t, when) in enumerate(zip(cu, (57, 63.5))):
        at(when, net.handed, t)
        for k in range(each):
            at(when + 1.3 * k, lift, i * each + k, 1)
    for j, (t, when) in enumerate(zip(cd, (69.5, 75.5, 81.5, 87.5))):
        at(when, net.handed, t)
        at(when, lower, j)
    for j, when in enumerate((80, 86, 95, 103)):
        at(when, finish, j)

    meet(net.neighbours())
    for _, _, act in sorted(steps, key=lambda step: step[:2]):
        act()
    net.drain()


def local(latents, offsets, levels, mod_table, rel_bias, w_qkv, w_out, w_up, w_down):
    count = lax.axis_size("win")
    batches, lat_rows, columns, features = latents.shape
    fits = count == 4 * LINE and lax.axis_size("groups") % 2 == 0 and columns == 2 * WIN
    if not (fits and lat_rows == WIN and batches == 3):
        return plain(
            latents, offsets, levels, mod_table, rel_bias, w_qkv, w_out, w_up, w_down
        )
    area = lat_rows * WIN
    own, moved = lat_rows * columns, 3 * area
    shards = (w_qkv, w_out, w_up, w_down)
    total = batches * own
    half_qkv, half_up = w_qkv.shape[1] // 2, w_up.shape[1] // 2
    inner = half_qkv // 3
    _, weight_sems = chunks_of([s.shape for s in shards], None)
    acts = PART + DOWN_CHUNKS
    vmem = pl.BlockSpec(memory_space=pltpu.VMEM)
    smem = pl.BlockSpec(memory_space=pltpu.SMEM)
    bf, f32 = jnp.bfloat16, jnp.float32
    found = pl.pallas_call(
        functools.partial(kernel, batches, area),
        out_shape=jax.ShapeDtypeStruct((total, features), bf),
        in_specs=[smem] * 2 + [vmem] * 7,
        out_specs=vmem,
        scratch_shapes=[
            pltpu.VMEM((features, half_qkv), bf),
            pltpu.VMEM((2 * inner, features), bf),
            pltpu.VMEM((features, half_up), bf),
            pltpu.VMEM((half_up, features), bf),
            pltpu.VMEM((2, w_qkv.shape[0], half_qkv), bf),
            pltpu.VMEM((2, w_up.shape[0], half_up), bf),
            pltpu.VMEM((batches, 6, features), f32),
            pltpu.VMEM((batches, moved, 4 * area), bf),
            pltpu.VMEM((batches, own, moved), bf),
            pltpu.VMEM((2, batches, own, features), bf),
            pltpu.VMEM((batches, 2, 4 * area, features), bf),
            pltpu.VMEM((batches, 2 * moved, features), bf),
            pltpu.VMEM((batches, 2 * moved, half_qkv), bf),
            pltpu.VMEM((batches, 2 * moved, inner), bf),
            pltpu.VMEM((batches, 2 * own, 2 * inner), bf),
            pltpu.VMEM((2, batches, own, features), bf),
            pltpu.VMEM((2, total, features), bf),
            pltpu.VMEM((2, total, half_up), bf),
            pltpu.VMEM((total, features), bf),
            pltpu.VMEM((total, features), bf),
            pltpu.VMEM((total, features), f32),
            pltpu.SemaphoreType.DMA((weight_sems,)),
            pltpu.SemaphoreType.DMA((weight_sems,)),
            pltpu.SemaphoreType.DMA((acts,)),
            pltpu.SemaphoreType.DMA((acts,)),
        ],
        compiler_params=pltpu.CompilerParams(
            collective_id=0, has_side_effects=True, vmem_limit_bytes=62 * 2**20
        ),
    )(offsets, levels, latents.reshape(total, features), mod_table, rel_bias, *shards)
    return found.reshape(latents.shape)


def solution(mesh):
    in_specs = (
        P("groups", None, "win", None),
        P("groups"),
        P("groups"),
        P(),
        P(),
        P("win", None),
        P("win", None),
        P("win", None),
        P("win", None),
    )
    out_specs = P("groups", None, "win", None)
    return jax.shard_map(local, mesh=mesh, in_specs=in_specs, out_specs=out_specs, check_vma=False)
```

```python
import functools

import jax
import jax.numpy as jnp
from jax import lax
from jax.experimental import pallas as pl
from jax.experimental.pallas import tpu as pltpu
from jax.sharding import PartitionSpec as P

HEADS = 6
HEAD_DIM = 128
WIN = 8
LEVELS = 32

MESH = pl.DeviceIdType.MESH
LINE = 4
LAT, STRIP, ATT, PART = 0, 3, 15, 18
UP_CHUNKS = 2
DOWN_SPLIT = (1, 2, 2, 1)
DOWN_CHUNKS = len(DOWN_SPLIT)


def under(condition, act):
    if condition is None:
        act()
    else:
        pl.when(condition)(act)


def both(one, other):
    return other if one is None else one & other


class Chunk:
    def __init__(self, full, depth, rows_by_y, first, width, by_rows, base):
        self.full, self.depth, self.rows_by_y = full, depth, rows_by_y
        self.first, self.width, self.by_rows, self.base = first, width, by_rows, base
        self.kinds = 2 if rows_by_y else 1
        self.count = 1 + 3 * LINE * self.kinds + 2 * LINE * self.kinds

    def region(self, z, y, c, h=None):
        at = (z * 2 + y) * 2 + c if self.rows_by_y else z * 2 + c
        start, size = at * self.depth, self.depth
        first, width = self.first, self.width
        if h is not None and self.by_rows:
            size = self.depth // 2
            start = start + h * size
        elif h is not None:
            width = self.width // 2
            first = pl.multiple_of(self.first + h * width, 128)
        return self.full.at[pl.ds(pl.multiple_of(start, 16), size), pl.ds(first, width)]

    def slot(self, kind, z, k=0):
        return self.base + 1 + kind * LINE * self.kinds + z * self.kinds + k

    def hand_slot(self, z, k, h):
        return self.base + 1 + 3 * LINE * self.kinds + (z * self.kinds + k) * 2 + h


UPWARD, DOWNWARD, ACROSS = 0, 1, 2


class Gather:
    def __init__(self, send, recv):
        self.send, self.recv = send, recv
        me = lax.axis_index("win")
        self.c = lax.rem(me, 2)
        self.y = lax.rem(me // 2, 2)
        self.z = me // 4
        self.g = lax.axis_index("groups")
        self.x = lax.rem(self.g, 2)
        up, down = lax.rem(self.z + 1, LINE), lax.rem(self.z + LINE - 1, LINE)
        self.to_up = {"win": self.place(up, self.y, self.c)}
        self.to_down = {"win": self.place(down, self.y, self.c)}
        self.to_y = {"win": self.place(self.z, 1 - self.y, self.c)}
        self.to_core = {"win": self.place(self.z, self.y, 1 - self.c)}
        self.to_x = {"groups": self.g + 1 - 2 * self.x}
        far = lax.rem(self.z + 2 * self.c + LINE - 1, LINE)
        self.to_far = {"win": self.place(far, self.y, 1 - self.c)}
        self.started = []

    def place(self, z, y, c):
        return (z * 2 + y) * 2 + c

    def neighbours(self):
        return [self.to_up, self.to_down, self.to_y, self.to_core, self.to_x, self.to_far]

    def copy(self, slot, src, dst, to):
        return pltpu.make_async_remote_copy(
            src_ref=src,
            dst_ref=dst,
            send_sem=self.send.at[slot],
            recv_sem=self.recv.at[slot],
            device_id=to,
            device_id_type=MESH,
        )

    def put(self, condition, make):
        under(condition, lambda: make().start())
        self.started.append((condition, make))

    def pass_on(self, condition, slot, part, to):
        self.put(condition, lambda: self.copy(slot, part(), part(), to))

    def arrive(self, condition, slot, part):
        under(condition, lambda: self.copy(slot, part(), part(), self.to_core).wait_recv())

    def side(self, k):
        return self.y if k == 0 else 1 - self.y

    def piece(self, t, z, k, h=None, c=None):
        return lambda: t.region(z, self.side(k), self.c if c is None else c, h)

    def y_send(self, t, source):
        self.put(None, lambda: self.copy(t.base, source(), self.piece(t, self.z, 0, self.x)(), self.to_y))

    def own(self, t):
        part = self.piece(t, self.z, 0, self.x)
        self.pass_on(self.z >= 1, t.slot(DOWNWARD, self.z), part, self.to_down)
        self.pass_on(self.z + 1 < LINE, t.slot(UPWARD, self.z), part, self.to_up)
        self.pass_on(None, t.hand_slot(self.z, 0, 0), self.piece(t, self.z, 0), self.to_core)

    def y_come(self, t):
        part = self.piece(t, self.z, 1, self.x)
        self.arrive(None, t.base, part)
        self.pass_on(self.z >= 1, t.slot(DOWNWARD, self.z, 1), part, self.to_down)
        self.pass_on(self.z + 1 < LINE, t.slot(UPWARD, self.z, 1), part, self.to_up)
        self.pass_on(None, t.slot(ACROSS, self.z, 1), part, self.to_x)
        self.pass_on(None, t.hand_slot(self.z, 1, self.x), part, self.to_core)

    def sources(self, d):
        if d == 0:
            return ((None, self.z),)
        return ((self.z >= d, self.z - d), (self.z + d < LINE, self.z + d))

    def z_come(self, t, d):
        ways = ((UPWARD, self.z + 1 < LINE, self.to_up), (DOWNWARD, self.z >= 1, self.to_down))
        for (there, z), (way, more, to) in zip(self.sources(d), ways):
            for k in range(t.kinds):
                part = self.piece(t, z, k, self.x)
                self.arrive(there, t.slot(way, z, k), part)
                if d < LINE - 1:
                    self.pass_on(there & more, t.slot(way, z, k), part, to)
                self.pass_on(there, t.slot(ACROSS, z, k), part, self.to_x)
                self.pass_on(there, t.hand_slot(z, k, self.x), part, self.to_core)

    def x_come(self, t, d):
        for there, z in self.sources(d):
            for k in range(1 if d == 0 else 0, t.kinds):
                part = self.piece(t, z, k, 1 - self.x)
                self.arrive(there, t.slot(ACROSS, z, k), part)
                self.pass_on(there, t.hand_slot(z, k, 1 - self.x), part, self.to_core)

    def handed(self, t):
        other = 1 - self.c
        self.arrive(None, t.hand_slot(self.z, 0, 0), self.piece(t, self.z, 0, None, other))
        for d in range(LINE):
            for there, z in self.sources(d):
                for k in range(1 if d == 0 else 0, t.kinds):
                    for h in range(2):
                        self.arrive(there, t.hand_slot(z, k, h), self.piece(t, z, k, h, other))

    def drain(self):
        for condition, make in self.started:
            under(condition, lambda make=make: make().wait_send())


def meet(neighbours):
    barrier = pltpu.get_barrier_semaphore()
    for to in neighbours:
        pl.semaphore_signal(barrier, inc=1, device_id=to, device_id_type=MESH)
    pl.semaphore_wait(barrier, len(neighbours))


def norm_rows(values_in):
    centre = values_in - jnp.mean(values_in, axis=-1, keepdims=True)
    spread = jnp.mean(centre * centre, axis=-1, keepdims=True)
    return centre * lax.rsqrt(spread + 1e-06)


def passed_along(shard, axis, by):
    length = lax.axis_size(axis)
    return lax.ppermute(shard, axis, [(i, (i + by) % length) for i in range(length)])


def cut(widened, starts, columns):
    return jnp.stack(
        [
            lax.dynamic_slice_in_dim(widened[m], starts[m], columns, 1)
            for m in range(widened.shape[0])
        ]
    )


def restore_grid(region, arrived, offsets, columns):
    return cut(jnp.concatenate([region, arrived], axis=2), offsets, columns)


def plain(latents, offsets, levels, mod_table, rel_bias, w_qkv, w_out, w_up, w_down):
    batches, lat_rows, columns, features = latents.shape
    inner = HEADS * HEAD_DIM
    per_dev = columns // WIN
    selector = (levels[:, None] == jnp.arange(LEVELS, dtype=jnp.int32)[None, :]).astype(
        jnp.bfloat16
    )
    modulation = jnp.dot(
        selector, mod_table.reshape(LEVELS, 6 * features), preferred_element_type=jnp.float32
    )
    modulation = modulation.reshape(batches, 6, 1, 1, features)
    stream = latents.astype(jnp.float32)
    normed = (norm_rows(stream) * (1.0 + modulation[:, 0]) + modulation[:, 1]).astype(jnp.bfloat16)
    arrived = passed_along(normed[:, :, columns - WIN :, :], "win", 1)
    widened = jnp.concatenate([arrived, normed], axis=2)
    rolled = cut(widened, WIN - offsets, columns)
    full_qkv = lax.all_gather(w_qkv, "win", axis=0, tiled=True)
    windows = rolled.reshape(batches, lat_rows, per_dev, WIN, features).transpose(0, 2, 1, 3, 4)
    windows = windows.reshape(-1, lat_rows * WIN, features)
    number = windows.shape[0]
    triple = jnp.dot(windows.reshape(-1, features), full_qkv, preferred_element_type=jnp.float32)
    triple = triple.astype(jnp.bfloat16).reshape(number, lat_rows * WIN, 3, HEADS, HEAD_DIM)
    scores = jnp.einsum(
        "wqhe,wkhe->whqk", triple[:, :, 0], triple[:, :, 1], preferred_element_type=jnp.float32
    )
    scores = scores * (1.0 / HEAD_DIM**0.5) + rel_bias[None]
    probs = jax.nn.softmax(scores, axis=-1).astype(jnp.bfloat16)
    attended = jnp.einsum(
        "whqk,wkhe->wqhe", probs, triple[:, :, 2], preferred_element_type=jnp.float32
    ).astype(jnp.bfloat16)
    attended = attended.reshape(batches, per_dev, lat_rows, WIN, inner).transpose(0, 2, 1, 3, 4)
    attended = attended.reshape(batches, lat_rows, columns, inner)
    full_out = lax.all_gather(w_out, "win", axis=0, tiled=True)
    returned = passed_along(attended[:, :, :WIN, :], "win", -1)
    restored = restore_grid(attended, returned, offsets, columns)
    projected = jnp.dot(restored.reshape(-1, inner), full_out, preferred_element_type=jnp.float32)
    projected = projected.reshape(batches, lat_rows, columns, features)
    middle = (stream + modulation[:, 2] * projected).astype(jnp.bfloat16)
    second = (
        norm_rows(middle.astype(jnp.float32)) * (1.0 + modulation[:, 3]) + modulation[:, 4]
    ).astype(jnp.bfloat16)
    full_up = lax.all_gather(w_up, "win", axis=0, tiled=True)
    hidden = jnp.dot(second.reshape(-1, features), full_up, preferred_element_type=jnp.float32)
    hidden = jax.nn.gelu(hidden, approximate=False).astype(jnp.bfloat16)
    full_down = lax.all_gather(w_down, "win", axis=0, tiled=True)
    lowered = jnp.dot(hidden, full_down, preferred_element_type=jnp.float32).reshape(
        batches, lat_rows, columns, features
    )
    return (middle.astype(jnp.float32) + modulation[:, 5] * lowered).astype(jnp.bfloat16)


def repeat(count, act):
    lax.fori_loop(0, count, lambda i, _: (act(i), 0)[1], 0)


def chunks_of(shapes, fulls):
    (q, o, u, d), base, made = shapes, 0, []

    def take(full, shape, split, rows_by_y, by_rows):
        nonlocal base
        unit, first = full[1] // sum(split), 0
        for part in split:
            ref = None if fulls is None else fulls[full[0]]
            made.append(Chunk(ref, shape[0], rows_by_y, first, part * unit, by_rows, base))
            base += made[-1].count
            first += part * unit

    take((0, q[1] // 2), q, (1,), True, True)
    take((1, o[1]), o, (1,), True, False)
    take((2, u[1] // 2), u, (1,) * UP_CHUNKS, True, True)
    take((3, d[1]), d, DOWN_SPLIT, False, True)
    return made, base


def kernel(
    batches, area, offsets_ref, levels_ref, lat_ref, table_ref, bias_ref, s0, s1, s2, s3, out_ref,
    f0, f1, f2, f3, a0, a2, mod, bias, scores, probs, gather_in, gather_out, lat, wide, wins, triple, heads, att, middle,
    second, hidden, part_out, part_in, part_own, send, recv, act_send, act_recv,
):
    features = lat_ref.shape[1]
    own = lat_ref.shape[0] // batches
    moved = gather_in.shape[1]
    inner = f0.shape[1] // 3
    pair_heads = inner // HEAD_DIM
    bf, f32 = jnp.bfloat16, jnp.float32
    chunks, _ = chunks_of((s0.shape, s1.shape, s2.shape, s3.shape), (f0, f1, f2, f3))
    cq, co, cu, cd = chunks[0], chunks[1], chunks[2 : 2 + UP_CHUNKS], chunks[2 + UP_CHUNKS :]
    net = Gather(send, recv)
    x, y, z, c = net.x, net.y, net.z, net.c
    other = 1 - y

    def activation(send_at, recv_at, src, dst, to):
        def make():
            return pltpu.make_async_remote_copy(
                src_ref=src(),
                dst_ref=dst(),
                send_sem=act_send.at[send_at],
                recv_sem=act_recv.at[recv_at],
                device_id=to,
                device_id_type=MESH,
            )

        net.put(None, make)

    def landed(recv_at, dst):
        pltpu.make_async_remote_copy(
            src_ref=dst,
            dst_ref=dst,
            send_sem=act_send.at[recv_at],
            recv_sem=act_recv.at[recv_at],
            device_id=net.to_core,
            device_id_type=MESH,
        ).wait_recv()

    def lay_qkv():
        for which in range(3):
            for k in range(2):
                first = (which * 2 + k) * inner
                a0[k, :, which * inner : (which + 1) * inner] = s0[:, first : first + inner]
        mine = net.place(z, y, c) * s0.shape[0]
        f0[pl.ds(pl.multiple_of(mine, 16), s0.shape[0]), :] = a0[y]

    def lay_out():
        mine = net.place(z, y, c) * s1.shape[0]
        f1[pl.ds(pl.multiple_of(mine, 16), s1.shape[0]), :] = s1[...]

    block = s3.shape[0] * 2

    def lay_up():
        for at in range(LINE):
            for k in range(2):
                first = (at * 2 + k) * block
                a2[k, :, at * block : (at + 1) * block] = s2[:, first : first + block]
        mine = net.place(z, y, c) * s2.shape[0]
        f2[pl.ds(pl.multiple_of(mine, 16), s2.shape[0]), :] = a2[y]

    def lay_down():
        mine = (z * 2 + c) * s3.shape[0]
        f3[pl.ds(pl.multiple_of(mine, 16), s3.shape[0]), :] = s3[...]

    def half_rows(ref, t):
        size = t.depth // 2
        rows = pl.ds(pl.multiple_of(x * size, 16), size)
        return lambda: ref.at[other, rows, pl.ds(t.first, t.width)]

    def send_lat(m):
        activation(
            LAT + m, LAT + m, lambda: lat_ref.at[pl.ds(m * own, own)], lambda: lat.at[y, m], net.to_y
        )

    def modulate():
        for m in range(batches):
            mod[m] = table_ref[levels_ref[m]].astype(f32)

    def make_moves():
        i = lax.broadcasted_iota(jnp.int32, (moved, wide.shape[2]), 0)
        j = lax.broadcasted_iota(jnp.int32, (moved, wide.shape[2]), 1)
        to_row, to_at = (i >> 3) & 7, ((i >> 6) << 3) + (i & 7)
        from_row, from_at = (j >> 3) & 7, ((j >> 6) << 3) + (j & 7)
        same = to_row == from_row
        k = lax.broadcasted_iota(jnp.int32, (own, moved), 0)
        n = lax.broadcasted_iota(jnp.int32, (own, moved), 1)
        back = (k >> 4) == ((n >> 3) & 7)
        back_at, rolled_at = k & 15, ((n >> 6) << 3) + (n & 7)
        for m in range(batches):
            by = offsets_ref[m]
            hit = same & (to_at + WIN - by == from_at)
            gather_in[m] = jnp.where(hit, 1.0, 0.0).astype(bf)
            hit = back & (back_at + by == rolled_at)
            gather_out[m] = jnp.where(hit, 1.0, 0.0).astype(bf)

    def copy_own():
        for m in range(batches):
            lat[y, m] = lat_ref[m * own : (m + 1) * own, :]

    def norm_tile(m, slot):
        def step(i):
            rows = lat[slot, m, i * 32 : (i + 1) * 32, :].astype(f32)
            value = norm_rows(rows) * (1.0 + mod[m, 0:1, :]) + mod[m, 1:2, :]
            value = value.reshape(2, 2, WIN, features)
            for half in range(2):
                start = (half + 1) * area + i * 16
                wide[m, slot, start : start + 16, :] = value[:, half].reshape(16, features).astype(bf)

        for i in range(own // 32):
            step(i)

    def strip(m, slot, at):
        return wide.at[m, slot, pl.ds(at * area, area)]

    def send_strips(m, slot):
        base = STRIP + m * 4
        low_slot = (1 - c) * (1 - slot) + c * slot
        low_z = lax.rem(z + LINE - (1 - c) * (1 - slot), LINE)
        activation(
            base + slot * 2, base + low_slot * 2 + 1,
            lambda: strip(m, slot, 1), lambda: strip(m, low_slot, 3),
            {"win": net.place(low_z, y, 1 - c)},
        )
        high_slot = (1 - c) * slot + c * (1 - slot)
        high_z = lax.rem(z + c * slot, LINE)
        activation(
            base + slot * 2 + 1, base + high_slot * 2,
            lambda: strip(m, slot, 2), lambda: strip(m, high_slot, 0),
            {"win": net.place(high_z, y, 1 - c)},
        )

    def norm_own(m):
        norm_tile(m, y)
        send_strips(m, y)

    def norm_other(m):
        landed(LAT + m, lat.at[other, m])
        norm_tile(m, other)
        send_strips(m, other)

    def windows(m):
        for slot in range(2):
            landed(STRIP + m * 4 + slot * 2, strip(m, slot, 0))
            landed(STRIP + m * 4 + slot * 2 + 1, strip(m, slot, 3))
        for slot in range(2):
            wins[m, slot * moved : (slot + 1) * moved, :] = jnp.dot(
                gather_in[m], wide[m, slot], preferred_element_type=f32
            ).astype(bf)

        def project(cols):
            triple[m, :, cols] = jnp.dot(
                wins[m], f0[:, cols], preferred_element_type=f32
            ).astype(bf)

        whole = f0.shape[1] // width
        repeat(whole, lambda i: project(columns(i)))
        project(slice(whole * width, f0.shape[1]))

    def make_bias():
        for head in range(pair_heads):
            one = bias_ref[y * pair_heads + head]
            rest = jnp.full(one.shape, -1e30, f32)
            bias[head, :area, :] = jnp.concatenate([one, rest], axis=1)
            bias[head, area:, :] = jnp.concatenate([rest, one], axis=1)

    def attend(m):
        pair = 2 * area
        spans = [
            (w * pair, head * HEAD_DIM, head)
            for w in range(moved // area)
            for head in range(pair_heads)
        ]

        def of(which, row, first):
            first = which * inner + first
            return triple[m, row : row + pair, first : first + HEAD_DIM]

        for i, (row, first, head) in enumerate(spans):
            found = lax.dot_general(
                of(0, row, first), of(1, row, first), (((1,), (1,)), ((), ())),
                preferred_element_type=f32,
            )
            scores[i * pair : (i + 1) * pair, :] = found * (1.0 / HEAD_DIM**0.5) + bias[head]
        group = pair_heads * pair
        for i in range(moved // area):
            rows = slice(i * group, (i + 1) * group)
            powers = scores[rows, :]
            powers = jnp.exp(powers - jnp.max(powers, axis=-1, keepdims=True))
            inverse = 1.0 / jnp.sum(powers, axis=-1, keepdims=True)
            probs[rows, :] = (powers * inverse).astype(bf)
        for i, (row, first, head) in enumerate(spans):
            heads[m, row : row + pair, first : first + HEAD_DIM] = jnp.dot(
                probs[i * pair : (i + 1) * pair, :], of(2, row, first), preferred_element_type=f32
            ).astype(bf)

        mine = pl.ds(pl.multiple_of(y * inner, 128), inner)
        for slot in range(2):
            att[m, pl.ds(slot * own, own), mine] = jnp.dot(
                gather_out[m], heads[m, slot * moved : (slot + 1) * moved, :],
                preferred_element_type=f32,
            ).astype(bf)
        activation(
            ATT + m, ATT + m, lambda: att.at[m, :, mine], lambda: att.at[m, :, mine], net.to_y
        )

    width = 256

    def columns(i):
        return pl.ds(pl.multiple_of(i * width, width), width)

    def settle(m):
        theirs = pl.ds(pl.multiple_of(other * inner, 128), inner)
        landed(ATT + m, att.at[m, :, theirs])

        def piece(i):
            cols = columns(i)
            found = jnp.dot(att[m], f1[:, cols], preferred_element_type=f32)
            for slot in range(2):
                change = mod[m, 2:3, cols] * found[slot * own : (slot + 1) * own]
                middle[slot, m, :, cols] = (lat[slot, m, :, cols].astype(f32) + change).astype(bf)

        repeat(features // width, piece)
        for slot in range(2):
            for i in range(own // 32):
                rows = middle[slot, m, i * 32 : (i + 1) * 32, :].astype(f32)
                value = norm_rows(rows) * (1.0 + mod[m, 3:4, :]) + mod[m, 4:5, :]
                start = m * own + i * 32
                second[slot, start : start + 32, :] = value.astype(bf)

    def lift(first, count):
        def piece(i):
            cols = columns(first + i)
            for slot in range(2):
                found = jnp.dot(second[slot], f2[:, cols], preferred_element_type=f32)
                found = 0.5 * found * (1.0 + lax.erf(found * (0.5**0.5)))
                hidden[slot, :, cols] = found.astype(bf)

        repeat(count, piece)

    def lower(j):
        cols = slice(cd[j].first, cd[j].first + cd[j].width)
        part_out[:, cols] = jnp.dot(
            hidden[other], f3[:, cols], preferred_element_type=f32
        ).astype(bf)
        activation(
            PART + j, PART + j, lambda: part_out.at[:, cols], lambda: part_in.at[:, cols], net.to_y
        )
        part_own[:, cols] = jnp.dot(hidden[y], f3[:, cols], preferred_element_type=f32)

    def finish(j):
        cols = slice(cd[j].first, cd[j].first + cd[j].width)
        landed(PART + j, part_in.at[:, cols])
        for m in range(batches):
            rows = slice(m * own, (m + 1) * own)
            change = part_own[rows, cols] + part_in[rows, cols].astype(f32)
            out_ref[rows, cols] = (
                middle[y, m, :, cols].astype(f32) + mod[m, 5:6, cols] * change
            ).astype(bf)

    steps = []

    def at(time, act, *args):
        steps.append((time, len(steps), functools.partial(act, *args)))

    def across(t, when):
        for d in range(0 if t.kinds == 2 else 1, LINE):
            at(when, net.x_come, t, d)

    at(0, lay_qkv)
    at(0, net.y_send, cq, half_rows(a0, cq))
    at(0.4, send_lat, 0)
    at(0.5, lay_out)
    at(0.5, net.y_send, co, net.piece(co, z, 0, x))
    at(0.6, send_lat, 1)
    at(0.6, send_lat, 2)
    at(0.7, lay_up)
    for t in cu:
        at(0.7, net.y_send, t, half_rows(a2, t))
    at(0.8, lay_down)
    at(0.9, copy_own)
    at(1, modulate)
    for m in range(batches):
        at(1 + 0.1 * m, norm_own, m)
    at(3.8, make_moves)
    at(3.9, make_bias)
    hops = ((7, 13, 19), (25, 29, 33), (37, 41, 45), (49, 53, 57)) + tuple(
        (60 + 6 * j, 62 + 6 * j, 64 + 6 * j) for j in range(DOWN_CHUNKS)
    )
    at(0.1, net.own, cq)
    at(4, net.y_come, cq)
    for i, t in enumerate(chunks):
        for d, when in enumerate(hops[i]):
            at(when, net.z_come, t, d + 1)
        if i + 1 < len(chunks):
            at(hops[i][0] - 0.1, net.own, chunks[i + 1])
            if chunks[i + 1].kinds == 2:
                at(hops[i][0] + 0.1, net.y_come, chunks[i + 1])
            across(t, hops[i + 1][0] + 0.05)
        else:
            across(t, hops[i][2] + 0.1)
    for m, when in enumerate((15, 25, 36.1)):
        at(when, norm_other, m)
    at(25.9, net.handed, cq)
    for m, when in enumerate((26, 31, 43)):
        at(when, windows, m)
        at(when + 0.1, attend, m)
    at(41.9, net.handed, co)
    for m, when in enumerate((42, 46, 56)):
        at(when, settle, m)
    each = f2.shape[1] // width // UP_CHUNKS
    for i, (t, when) in enumerate(zip(cu, (57, 63.5))):
        at(when, net.handed, t)
        for k in range(each):
            at(when + 1.3 * k, lift, i * each + k, 1)
    for j, (t, when) in enumerate(zip(cd, (66.5, 72.5, 78.5, 84.5))):
        at(when, net.handed, t)
        at(when, lower, j)
    for j, when in enumerate((80, 86, 95, 103)):
        at(when, finish, j)

    meet(net.neighbours())
    for _, _, act in sorted(steps, key=lambda step: step[:2]):
        act()
    net.drain()


def local(latents, offsets, levels, mod_table, rel_bias, w_qkv, w_out, w_up, w_down):
    count = lax.axis_size("win")
    batches, lat_rows, columns, features = latents.shape
    fits = count == 4 * LINE and lax.axis_size("groups") % 2 == 0 and columns == 2 * WIN
    if not (fits and lat_rows == WIN and batches == 3):
        return plain(
            latents, offsets, levels, mod_table, rel_bias, w_qkv, w_out, w_up, w_down
        )
    area = lat_rows * WIN
    own, moved = lat_rows * columns, 3 * area
    shards = (w_qkv, w_out, w_up, w_down)
    total = batches * own
    half_qkv, half_up = w_qkv.shape[1] // 2, w_up.shape[1] // 2
    inner = half_qkv // 3
    _, weight_sems = chunks_of([s.shape for s in shards], None)
    acts = PART + DOWN_CHUNKS
    vmem = pl.BlockSpec(memory_space=pltpu.VMEM)
    smem = pl.BlockSpec(memory_space=pltpu.SMEM)
    bf, f32 = jnp.bfloat16, jnp.float32
    found = pl.pallas_call(
        functools.partial(kernel, batches, area),
        out_shape=jax.ShapeDtypeStruct((total, features), bf),
        in_specs=[smem] * 2 + [vmem] * 7,
        out_specs=vmem,
        scratch_shapes=[
            pltpu.VMEM((features, half_qkv), bf),
            pltpu.VMEM((2 * inner, features), bf),
            pltpu.VMEM((features, half_up), bf),
            pltpu.VMEM((half_up, features), bf),
            pltpu.VMEM((2, w_qkv.shape[0], half_qkv), bf),
            pltpu.VMEM((2, w_up.shape[0], half_up), bf),
            pltpu.VMEM((batches, 6, features), f32),
            pltpu.VMEM((HEADS // 2, 2 * area, 2 * area), f32),
            pltpu.VMEM((HEADS // 2 * 6 * area, 2 * area), f32),
            pltpu.VMEM((HEADS // 2 * 6 * area, 2 * area), bf),
            pltpu.VMEM((batches, moved, 4 * area), bf),
            pltpu.VMEM((batches, own, moved), bf),
            pltpu.VMEM((2, batches, own, features), bf),
            pltpu.VMEM((batches, 2, 4 * area, features), bf),
            pltpu.VMEM((batches, 2 * moved, features), bf),
            pltpu.VMEM((batches, 2 * moved, half_qkv), bf),
            pltpu.VMEM((batches, 2 * moved, inner), bf),
            pltpu.VMEM((batches, 2 * own, 2 * inner), bf),
            pltpu.VMEM((2, batches, own, features), bf),
            pltpu.VMEM((2, total, features), bf),
            pltpu.VMEM((2, total, half_up), bf),
            pltpu.VMEM((total, features), bf),
            pltpu.VMEM((total, features), bf),
            pltpu.VMEM((total, features), f32),
            pltpu.SemaphoreType.DMA((weight_sems,)),
            pltpu.SemaphoreType.DMA((weight_sems,)),
            pltpu.SemaphoreType.DMA((acts,)),
            pltpu.SemaphoreType.DMA((acts,)),
        ],
        compiler_params=pltpu.CompilerParams(
            collective_id=0, has_side_effects=True, vmem_limit_bytes=62 * 2**20
        ),
    )(offsets, levels, latents.reshape(total, features), mod_table, rel_bias, *shards)
    return found.reshape(latents.shape)


def solution(mesh):
    in_specs = (
        P("groups", None, "win", None),
        P("groups"),
        P("groups"),
        P(),
        P(),
        P("win", None),
        P("win", None),
        P("win", None),
        P("win", None),
    )
    out_specs = P("groups", None, "win", None)
    return jax.shard_map(local, mesh=mesh, in_specs=in_specs, out_specs=out_specs, check_vma=False)
```

```python
import functools

import jax
import jax.numpy as jnp
from jax import lax
from jax.experimental import pallas as pl
from jax.experimental.pallas import tpu as pltpu
from jax.sharding import PartitionSpec as P

HEADS = 6
HEAD_DIM = 128
WIN = 8
LEVELS = 32

MESH = pl.DeviceIdType.MESH
LINE = 4
LAT, STRIP, ATT, PART = 0, 3, 15, 18
PARTS = 6
UP_CHUNKS = 2
DOWN_SPLIT = (1, 2, 2, 1)
DOWN_CHUNKS = len(DOWN_SPLIT)


ORDER = (
    11, 12, 14, 0, 1, 10, 5, 2, 3, 7, 18, 20, 24, 90, 19, 9, 21, 32, 33, 4, 40, 34, 25, 13, 23,
    26, 8, 27, 15, 22, 6, 31, 41, 44, 79, 37, 28, 38, 42, 54, 16, 39, 116, 29, 52, 43, 17, 53,
    30, 35, 55, 45, 67, 36, 58, 48, 68, 66, 50, 65, 49, 46, 47, 103, 60, 56, 57, 59, 71, 69, 70,
    80, 78, 51, 61, 64, 74, 81, 77, 83, 88, 62, 91, 82, 72, 73, 89, 63, 75, 87, 92, 76, 84, 85,
    99, 102, 93, 94, 104, 96, 117, 98, 105, 101, 97, 95, 86, 106, 107, 111, 110, 112, 109, 115,
    100, 118, 124, 108, 119, 113, 120, 121, 114, 123, 122, 125,
)


def under(condition, act):
    if condition is None:
        act()
    else:
        pl.when(condition)(act)


def both(one, other):
    return other if one is None else one & other


class Chunk:
    count = 1 + 4 * LINE

    def __init__(self, full, depth, by_y, first, width, by_rows, base):
        self.full, self.depth, self.by_y = full, depth, by_y
        self.first, self.width, self.by_rows, self.base = first, width, by_rows, base

    def region(self, z, c, h=None, y=None):
        start, size = 0, self.depth
        first, width = self.first, self.width
        if h is not None and self.by_rows:
            size = self.depth // 2
            start = pl.multiple_of(h * size, 16)
        elif h is not None:
            width = self.width // 2
            first = pl.multiple_of(self.first + h * width, 128)
        rows, cols = pl.ds(start, size), pl.ds(first, width)
        if not self.by_y:
            return self.full.at[z, c, rows, cols]
        if y is None:
            return self.full.at[z, :, c, rows, cols]
        return self.full.at[z, y, c, rows, cols]

    def slot(self, kind, z):
        return self.base + 1 + kind * LINE + z


def flat(ref, cols):
    part = ref[(slice(None),) * (len(ref.shape) - 1) + (cols,)]
    return part.reshape(-1, part.shape[-1])


UPWARD, DOWNWARD, ACROSS, HAND = range(4)


class Gather:
    def __init__(self, send, recv):
        self.send, self.recv = send, recv
        me = lax.axis_index("win")
        self.c = lax.rem(me, 2)
        self.y = lax.rem(me // 2, 2)
        self.z = me // 4
        self.g = lax.axis_index("groups")
        self.x = lax.rem(self.g, 2)
        up, down = lax.rem(self.z + 1, LINE), lax.rem(self.z + LINE - 1, LINE)
        self.to_up = {"win": self.place(up, self.y, self.c)}
        self.to_down = {"win": self.place(down, self.y, self.c)}
        self.to_y = {"win": self.place(self.z, 1 - self.y, self.c)}
        self.to_core = {"win": self.place(self.z, self.y, 1 - self.c)}
        self.to_x = {"groups": self.g + 1 - 2 * self.x}
        far = lax.rem(self.z + 2 * self.c + LINE - 1, LINE)
        self.to_far = {"win": self.place(far, self.y, 1 - self.c)}
        self.started = []

    def place(self, z, y, c):
        return (z * 2 + y) * 2 + c

    def neighbours(self):
        return [self.to_up, self.to_down, self.to_y, self.to_core, self.to_x, self.to_far]

    def copy(self, slot, src, dst, to):
        return pltpu.make_async_remote_copy(
            src_ref=src,
            dst_ref=dst,
            send_sem=self.send.at[slot],
            recv_sem=self.recv.at[slot],
            device_id=to,
            device_id_type=MESH,
        )

    def put(self, condition, make):
        under(condition, lambda: make().start())
        self.started.append((condition, make))

    def pass_on(self, condition, slot, part, to):
        self.put(condition, lambda: self.copy(slot, part(), part(), to))

    def arrive(self, condition, slot, part):
        under(condition, lambda: self.copy(slot, part(), part(), self.to_core).wait_recv())

    def y_send(self, t, source):
        part = lambda: t.region(self.z, self.c, self.x, self.y)
        self.put(None, lambda: self.copy(t.base, source(), part(), self.to_y))

    def own(self, t):
        part = lambda: t.region(self.z, self.c, self.x)
        self.pass_on(self.z >= 1, t.slot(DOWNWARD, self.z), part, self.to_down)
        self.pass_on(self.z + 1 < LINE, t.slot(UPWARD, self.z), part, self.to_up)

    def y_come(self, t):
        part = lambda: t.region(self.z, self.c, self.x, 1 - self.y)
        self.arrive(None, t.base, part)
        self.own(t)
        self.pass_on(None, t.slot(ACROSS, self.z), part, self.to_x)

    def sources(self, d):
        if d == 0:
            return ((None, self.z),)
        return ((self.z >= d, self.z - d), (self.z + d < LINE, self.z + d))

    def z_come(self, t, d):
        ways = ((UPWARD, self.z + 1 < LINE, self.to_up), (DOWNWARD, self.z >= 1, self.to_down))
        for (there, z), (way, more, to) in zip(self.sources(d), ways):
            part = lambda z=z: t.region(z, self.c, self.x)
            self.arrive(there, t.slot(way, z), part)
            if d < LINE - 1:
                self.pass_on(there & more, t.slot(way, z), part, to)
            self.pass_on(there, t.slot(ACROSS, z), part, self.to_x)

    def x_come(self, t, d):
        for there, z in self.sources(d):
            if d > 0:
                self.arrive(there, t.slot(ACROSS, z), lambda z=z: t.region(z, self.c, 1 - self.x))
            elif t.by_y:
                part = lambda: t.region(self.z, self.c, 1 - self.x, 1 - self.y)
                self.arrive(None, t.slot(ACROSS, self.z), part)
            self.pass_on(there, t.slot(HAND, z), lambda z=z: t.region(z, self.c), self.to_core)

    def handed(self, t):
        for z in range(LINE):
            self.arrive(None, t.slot(HAND, z), lambda z=z: t.region(z, 1 - self.c))

    def drain(self):
        for condition, make in self.started:
            under(condition, lambda make=make: make().wait_send())


def meet(neighbours):
    barrier = pltpu.get_barrier_semaphore()
    for to in neighbours:
        pl.semaphore_signal(barrier, inc=1, device_id=to, device_id_type=MESH)
    pl.semaphore_wait(barrier, len(neighbours))


def norm_rows(values_in):
    centre = values_in - jnp.mean(values_in, axis=-1, keepdims=True)
    spread = jnp.mean(centre * centre, axis=-1, keepdims=True)
    return centre * lax.rsqrt(spread + 1e-06)


def passed_along(shard, axis, by):
    length = lax.axis_size(axis)
    return lax.ppermute(shard, axis, [(i, (i + by) % length) for i in range(length)])


def cut(widened, starts, columns):
    return jnp.stack(
        [
            lax.dynamic_slice_in_dim(widened[m], starts[m], columns, 1)
            for m in range(widened.shape[0])
        ]
    )


def restore_grid(region, arrived, offsets, columns):
    return cut(jnp.concatenate([region, arrived], axis=2), offsets, columns)


def plain(latents, offsets, levels, mod_table, rel_bias, w_qkv, w_out, w_up, w_down):
    batches, lat_rows, columns, features = latents.shape
    inner = HEADS * HEAD_DIM
    per_dev = columns // WIN
    selector = (levels[:, None] == jnp.arange(LEVELS, dtype=jnp.int32)[None, :]).astype(
        jnp.bfloat16
    )
    modulation = jnp.dot(
        selector, mod_table.reshape(LEVELS, 6 * features), preferred_element_type=jnp.float32
    )
    modulation = modulation.reshape(batches, 6, 1, 1, features)
    stream = latents.astype(jnp.float32)
    normed = (norm_rows(stream) * (1.0 + modulation[:, 0]) + modulation[:, 1]).astype(jnp.bfloat16)
    arrived = passed_along(normed[:, :, columns - WIN :, :], "win", 1)
    widened = jnp.concatenate([arrived, normed], axis=2)
    rolled = cut(widened, WIN - offsets, columns)
    full_qkv = lax.all_gather(w_qkv, "win", axis=0, tiled=True)
    windows = rolled.reshape(batches, lat_rows, per_dev, WIN, features).transpose(0, 2, 1, 3, 4)
    windows = windows.reshape(-1, lat_rows * WIN, features)
    number = windows.shape[0]
    triple = jnp.dot(windows.reshape(-1, features), full_qkv, preferred_element_type=jnp.float32)
    triple = triple.astype(jnp.bfloat16).reshape(number, lat_rows * WIN, 3, HEADS, HEAD_DIM)
    scores = jnp.einsum(
        "wqhe,wkhe->whqk", triple[:, :, 0], triple[:, :, 1], preferred_element_type=jnp.float32
    )
    scores = scores * (1.0 / HEAD_DIM**0.5) + rel_bias[None]
    probs = jax.nn.softmax(scores, axis=-1).astype(jnp.bfloat16)
    attended = jnp.einsum(
        "whqk,wkhe->wqhe", probs, triple[:, :, 2], preferred_element_type=jnp.float32
    ).astype(jnp.bfloat16)
    attended = attended.reshape(batches, per_dev, lat_rows, WIN, inner).transpose(0, 2, 1, 3, 4)
    attended = attended.reshape(batches, lat_rows, columns, inner)
    full_out = lax.all_gather(w_out, "win", axis=0, tiled=True)
    returned = passed_along(attended[:, :, :WIN, :], "win", -1)
    restored = restore_grid(attended, returned, offsets, columns)
    projected = jnp.dot(restored.reshape(-1, inner), full_out, preferred_element_type=jnp.float32)
    projected = projected.reshape(batches, lat_rows, columns, features)
    middle = (stream + modulation[:, 2] * projected).astype(jnp.bfloat16)
    second = (
        norm_rows(middle.astype(jnp.float32)) * (1.0 + modulation[:, 3]) + modulation[:, 4]
    ).astype(jnp.bfloat16)
    full_up = lax.all_gather(w_up, "win", axis=0, tiled=True)
    hidden = jnp.dot(second.reshape(-1, features), full_up, preferred_element_type=jnp.float32)
    hidden = jax.nn.gelu(hidden, approximate=False).astype(jnp.bfloat16)
    full_down = lax.all_gather(w_down, "win", axis=0, tiled=True)
    lowered = jnp.dot(hidden, full_down, preferred_element_type=jnp.float32).reshape(
        batches, lat_rows, columns, features
    )
    return (middle.astype(jnp.float32) + modulation[:, 5] * lowered).astype(jnp.bfloat16)


def repeat(count, act):
    lax.fori_loop(0, count, lambda i, _: (act(i), 0)[1], 0)


def chunks_of(shapes, fulls):
    (q, o, u, d), base, made = shapes, 0, []

    def take(full, shape, split, by_y, by_rows):
        nonlocal base
        unit, first = full[1] // sum(split), 0
        for part in split:
            ref = None if fulls is None else fulls[full[0]]
            made.append(Chunk(ref, shape[0], by_y, first, part * unit, by_rows, base))
            base += Chunk.count
            first += part * unit

    take((0, q[1] // 2), q, (1,), True, True)
    take((1, o[1]), o, (1,), True, False)
    take((2, u[1] // 2), u, (1,) * UP_CHUNKS, True, True)
    take((3, d[1]), d, DOWN_SPLIT, False, True)
    return made, base


def kernel(
    batches, area, offsets_ref, levels_ref, lat_ref, table_ref, bias_ref, s0, s1, s2, s3, out_ref,
    f0, f1, f2, f3, a0, a2, mod, bias, scores, probs, gather_in, gather_out, lat, wide, wins, triple, heads, att, middle,
    second, hidden, part_out, part_in, part_own, send, recv, act_send, act_recv,
):
    features = lat_ref.shape[1]
    own = lat_ref.shape[0] // batches
    moved = gather_in.shape[1]
    inner = f0.shape[-1] // 3
    pair_heads = inner // HEAD_DIM
    bf, f32 = jnp.bfloat16, jnp.float32
    chunks, _ = chunks_of((s0.shape, s1.shape, s2.shape, s3.shape), (f0, f1, f2, f3))
    cq, co, cu, cd = chunks[0], chunks[1], chunks[2 : 2 + UP_CHUNKS], chunks[2 + UP_CHUNKS :]
    net = Gather(send, recv)
    x, y, z, c = net.x, net.y, net.z, net.c
    other = 1 - y

    def activation(send_at, recv_at, src, dst, to):
        def make():
            return pltpu.make_async_remote_copy(
                src_ref=src(),
                dst_ref=dst(),
                send_sem=act_send.at[send_at],
                recv_sem=act_recv.at[recv_at],
                device_id=to,
                device_id_type=MESH,
            )

        net.put(None, make)

    def landed(recv_at, dst):
        pltpu.make_async_remote_copy(
            src_ref=dst,
            dst_ref=dst,
            send_sem=act_send.at[recv_at],
            recv_sem=act_recv.at[recv_at],
            device_id=net.to_core,
            device_id_type=MESH,
        ).wait_recv()

    def lay_qkv():
        for which in range(3):
            for k in range(2):
                first = (which * 2 + k) * inner
                a0[k, :, which * inner : (which + 1) * inner] = s0[:, first : first + inner]
        f0[z, y, c] = a0[y]

    def lay_out():
        f1[z, y, c] = s1[...]

    block = s3.shape[0] * 2

    def lay_up():
        for at in range(LINE):
            for k in range(2):
                first = (at * 2 + k) * block
                a2[k, :, at * block : (at + 1) * block] = s2[:, first : first + block]
        f2[z, y, c] = a2[y]

    def lay_down():
        f3[z, c] = s3[...]

    def half_rows(ref, t):
        size = t.depth // 2
        rows = pl.ds(pl.multiple_of(x * size, 16), size)
        return lambda: ref.at[other, rows, pl.ds(t.first, t.width)]

    def send_lat(m):
        activation(
            LAT + m, LAT + m, lambda: lat_ref.at[pl.ds(m * own, own)], lambda: lat.at[y, m], net.to_y
        )

    def modulate():
        shape = (8, table_ref.shape[1])
        row = lax.broadcasted_iota(jnp.int32, shape, 0)
        level = lax.broadcasted_iota(jnp.int32, shape, 1)
        hit = (row == 0) & (level == levels_ref[0])
        for m in range(1, batches):
            hit = hit | ((row == m) & (level == levels_ref[m]))
        pick = jnp.where(hit, 1.0, 0.0).astype(bf)
        for k in range(table_ref.shape[0]):
            found = jnp.dot(pick, table_ref[k], preferred_element_type=f32)
            for m in range(batches):
                mod[m, k : k + 1, :] = found[m : m + 1, :]

    def make_moves():
        i = lax.broadcasted_iota(jnp.int32, (moved, wide.shape[2]), 0)
        j = lax.broadcasted_iota(jnp.int32, (moved, wide.shape[2]), 1)
        to_row, to_at = (i >> 3) & 7, ((i >> 6) << 3) + (i & 7)
        from_row, from_at = (j >> 3) & 7, ((j >> 6) << 3) + (j & 7)
        same = to_row == from_row
        k = lax.broadcasted_iota(jnp.int32, (own, moved), 0)
        n = lax.broadcasted_iota(jnp.int32, (own, moved), 1)
        back = (k >> 4) == ((n >> 3) & 7)
        back_at, rolled_at = k & 15, ((n >> 6) << 3) + (n & 7)
        for m in range(batches):
            by = offsets_ref[m]
            hit = same & (to_at + WIN - by == from_at)
            gather_in[m] = jnp.where(hit, 1.0, 0.0).astype(bf)
            hit = back & (back_at + by == rolled_at)
            gather_out[m] = jnp.where(hit, 1.0, 0.0).astype(bf)

    def copy_own():
        for m in range(batches):
            lat[y, m] = lat_ref[m * own : (m + 1) * own, :]

    def norm_tile(m, slot):
        def step(i):
            rows = lat[slot, m, i * 32 : (i + 1) * 32, :].astype(f32)
            value = norm_rows(rows) * (1.0 + mod[m, 0:1, :]) + mod[m, 1:2, :]
            value = value.reshape(2, 2, WIN, features)
            for half in range(2):
                start = (half + 1) * area + i * 16
                wide[m, slot, start : start + 16, :] = value[:, half].reshape(16, features).astype(bf)

        for i in range(own // 32):
            step(i)

    def strip(m, slot, at):
        return wide.at[m, slot, pl.ds(at * area, area)]

    def send_strips(m, slot):
        base = STRIP + m * 4
        low_slot = (1 - c) * (1 - slot) + c * slot
        low_z = lax.rem(z + LINE - (1 - c) * (1 - slot), LINE)
        activation(
            base + slot * 2, base + low_slot * 2 + 1,
            lambda: strip(m, slot, 1), lambda: strip(m, low_slot, 3),
            {"win": net.place(low_z, y, 1 - c)},
        )
        high_slot = (1 - c) * slot + c * (1 - slot)
        high_z = lax.rem(z + c * slot, LINE)
        activation(
            base + slot * 2 + 1, base + high_slot * 2,
            lambda: strip(m, slot, 2), lambda: strip(m, high_slot, 0),
            {"win": net.place(high_z, y, 1 - c)},
        )

    def norm_own(m):
        norm_tile(m, y)
        send_strips(m, y)

    def norm_other(m):
        landed(LAT + m, lat.at[other, m])
        norm_tile(m, other)
        send_strips(m, other)

    def windows(m):
        for slot in range(2):
            landed(STRIP + m * 4 + slot * 2, strip(m, slot, 0))
            landed(STRIP + m * 4 + slot * 2 + 1, strip(m, slot, 3))
        for slot in range(2):
            wins[m, slot * moved : (slot + 1) * moved, :] = jnp.dot(
                gather_in[m], wide[m, slot], preferred_element_type=f32
            ).astype(bf)

        def project(cols):
            triple[m, :, cols] = jnp.dot(
                wins[m], flat(f0, cols), preferred_element_type=f32
            ).astype(bf)

        whole = f0.shape[-1] // width
        repeat(whole, lambda i: project(columns(i)))
        project(slice(whole * width, f0.shape[-1]))

    def make_bias():
        for head in range(pair_heads):
            one = bias_ref[y * pair_heads + head]
            rest = jnp.full(one.shape, -1e30, f32)
            bias[head, :area, :] = jnp.concatenate([one, rest], axis=1)
            bias[head, area:, :] = jnp.concatenate([rest, one], axis=1)

    def attend(m):
        pair = 2 * area
        spans = [
            (w * pair, head * HEAD_DIM, head)
            for w in range(moved // area)
            for head in range(pair_heads)
        ]

        def of(which, row, first):
            first = which * inner + first
            return triple[m, row : row + pair, first : first + HEAD_DIM]

        for i, (row, first, head) in enumerate(spans):
            found = lax.dot_general(
                of(0, row, first), of(1, row, first), (((1,), (1,)), ((), ())),
                preferred_element_type=f32,
            )
            scores[i * pair : (i + 1) * pair, :] = found * (1.0 / HEAD_DIM**0.5) + bias[head]
        group = pair_heads * pair
        for i in range(moved // area):
            rows = slice(i * group, (i + 1) * group)
            powers = scores[rows, :]
            powers = jnp.exp(powers - jnp.max(powers, axis=-1, keepdims=True))
            inverse = 1.0 / jnp.sum(powers, axis=-1, keepdims=True)
            probs[rows, :] = (powers * inverse).astype(bf)
        for i, (row, first, head) in enumerate(spans):
            heads[m, row : row + pair, first : first + HEAD_DIM] = jnp.dot(
                probs[i * pair : (i + 1) * pair, :], of(2, row, first), preferred_element_type=f32
            ).astype(bf)

        mine = pl.ds(pl.multiple_of(y * inner, 128), inner)
        for slot in range(2):
            att[m, pl.ds(slot * own, own), mine] = jnp.dot(
                gather_out[m], heads[m, slot * moved : (slot + 1) * moved, :],
                preferred_element_type=f32,
            ).astype(bf)
        activation(
            ATT + m, ATT + m, lambda: att.at[m, :, mine], lambda: att.at[m, :, mine], net.to_y
        )

    width = 256

    def columns(i):
        return pl.ds(pl.multiple_of(i * width, width), width)

    def settle(m):
        theirs = pl.ds(pl.multiple_of(other * inner, 128), inner)
        landed(ATT + m, att.at[m, :, theirs])

        def piece(i):
            cols = columns(i)
            found = jnp.dot(att[m], flat(f1, cols), preferred_element_type=f32)
            for slot in range(2):
                change = mod[m, 2:3, cols] * found[slot * own : (slot + 1) * own]
                middle[slot, m, :, cols] = (lat[slot, m, :, cols].astype(f32) + change).astype(bf)

        repeat(features // width, piece)
        for slot in range(2):
            for i in range(own // 32):
                rows = middle[slot, m, i * 32 : (i + 1) * 32, :].astype(f32)
                value = norm_rows(rows) * (1.0 + mod[m, 3:4, :]) + mod[m, 4:5, :]
                start = m * own + i * 32
                second[slot, start : start + 32, :] = value.astype(bf)

    def lift(first, count):
        def piece(i):
            cols = columns(first + i)
            for slot in range(2):
                found = jnp.dot(second[slot], flat(f2, cols), preferred_element_type=f32)
                found = 0.5 * found * (1.0 + lax.erf(found * (0.5**0.5)))
                hidden[slot, :, cols] = found.astype(bf)

        repeat(count, piece)

    part = features // PARTS

    def lower(j):
        cols = slice(j * part, (j + 1) * part)
        part_out[:, cols] = jnp.dot(
            hidden[other], flat(f3, cols), preferred_element_type=f32
        ).astype(bf)
        activation(
            PART + j, PART + j, lambda: part_out.at[:, cols], lambda: part_in.at[:, cols], net.to_y
        )

    def lower_own(j):
        cols = slice(j * part, (j + 1) * part)
        part_own[:, cols] = jnp.dot(hidden[y], flat(f3, cols), preferred_element_type=f32)

    def finish(j):
        cols = slice(j * part, (j + 1) * part)
        landed(PART + j, part_in.at[:, cols])
        for m in range(batches):
            rows = slice(m * own, (m + 1) * own)
            change = part_own[rows, cols] + part_in[rows, cols].astype(f32)
            out_ref[rows, cols] = (
                middle[y, m, :, cols].astype(f32) + mod[m, 5:6, cols] * change
            ).astype(bf)

    steps = []

    def at(time, act, *args):
        steps.append((time, len(steps), functools.partial(act, *args)))

    def across(t, when):
        for d in range(LINE):
            at(when, net.x_come, t, d)

    at(0, lay_qkv)
    at(0, net.y_send, cq, half_rows(a0, cq))
    at(0.5, lay_out)
    at(0.5, net.y_send, co, lambda: co.region(z, c, x, y))
    at(0.5, send_lat, 0)
    at(0.6, lay_up)
    at(0.6, net.y_send, cu[0], half_rows(a2, cu[0]))
    at(0.7, send_lat, 1)
    at(0.7, net.y_send, cu[1], half_rows(a2, cu[1]))
    at(0.8, send_lat, 2)
    at(0.8, lay_down)
    at(0.9, copy_own)
    at(1, modulate)
    for m in range(batches):
        at(1 + 0.1 * m, norm_own, m)
    at(3.8, make_moves)
    at(3.9, make_bias)
    hops = ((7, 13, 19), (25, 29, 33), (37, 41, 45), (49, 53, 57)) + (
        (60, 62, 64), (65, 66, 68), (72, 74, 77), (80, 82, 85)
    )
    at(4, net.y_come, cq)
    for i, t in enumerate(chunks):
        for d, when in enumerate(hops[i]):
            at(when, net.z_come, t, d + 1)
        if i == 0:
            across(t, 22.5)
        elif i + 1 < len(chunks):
            across(t, hops[i + 1][0] + 0.05)
        else:
            across(t, hops[i][2] + 0.1)
        if i + 1 < len(chunks):
            at(hops[i][0] - 0.1, net.y_come if chunks[i + 1].by_y else net.own, chunks[i + 1])
    for m, when in enumerate((15, 26.5, 38)):
        at(when, norm_other, m)
    at(22.9, net.handed, cq)
    for m, when in enumerate((23, 31, 43)):
        at(when, windows, m)
        at(when + 0.1, attend, m)
    at(41.9, net.handed, co)
    for m, when in enumerate((42, 46, 56)):
        at(when, settle, m)
    each = f2.shape[-1] // width // UP_CHUNKS
    for i, (t, when) in enumerate(zip(cu, (57, 63.5))):
        at(when, net.handed, t)
        for k in range(each):
            at(when + 0.5 * k, lift, i * each + k, 1)
    done = 0
    for t, when in zip(cd, (66.5, 73, 81, 86)):
        at(when, net.handed, t)
        for k in range(t.width // part):
            at(when + 0.1, lower, done)
            at(when + 0.2, lower_own, done)
            done += 1
    for j, when in enumerate((74, 82, 82.5, 87, 88, 89)):
        at(when, finish, j)

    meet(net.neighbours())
    listed = sorted(steps, key=lambda step: step[:2])
    for i in ORDER:
        listed[i][2]()
    net.drain()


def local(latents, offsets, levels, mod_table, rel_bias, w_qkv, w_out, w_up, w_down):
    count = lax.axis_size("win")
    batches, lat_rows, columns, features = latents.shape
    fits = count == 4 * LINE and lax.axis_size("groups") % 2 == 0 and columns == 2 * WIN
    if not (fits and lat_rows == WIN and batches == 3):
        return plain(
            latents, offsets, levels, mod_table, rel_bias, w_qkv, w_out, w_up, w_down
        )
    area = lat_rows * WIN
    own, moved = lat_rows * columns, 3 * area
    shards = (w_qkv, w_out, w_up, w_down)
    total = batches * own
    half_qkv, half_up = w_qkv.shape[1] // 2, w_up.shape[1] // 2
    inner = half_qkv // 3
    _, weight_sems = chunks_of([s.shape for s in shards], None)
    acts = PART + PARTS
    vmem = pl.BlockSpec(memory_space=pltpu.VMEM)
    smem = pl.BlockSpec(memory_space=pltpu.SMEM)
    bf, f32 = jnp.bfloat16, jnp.float32
    found = pl.pallas_call(
        functools.partial(kernel, batches, area),
        out_shape=jax.ShapeDtypeStruct((total, features), bf),
        in_specs=[smem] * 2 + [vmem] * 7,
        out_specs=vmem,
        scratch_shapes=[
            pltpu.VMEM((LINE, 2, 2, w_qkv.shape[0], half_qkv), bf),
            pltpu.VMEM((LINE, 2, 2, w_out.shape[0], features), bf),
            pltpu.VMEM((LINE, 2, 2, w_up.shape[0], half_up), bf),
            pltpu.VMEM((LINE, 2, w_down.shape[0], features), bf),
            pltpu.VMEM((2, w_qkv.shape[0], half_qkv), bf),
            pltpu.VMEM((2, w_up.shape[0], half_up), bf),
            pltpu.VMEM((batches, 6, features), f32),
            pltpu.VMEM((HEADS // 2, 2 * area, 2 * area), f32),
            pltpu.VMEM((HEADS // 2 * 6 * area, 2 * area), f32),
            pltpu.VMEM((HEADS // 2 * 6 * area, 2 * area), bf),
            pltpu.VMEM((batches, moved, 4 * area), bf),
            pltpu.VMEM((batches, own, moved), bf),
            pltpu.VMEM((2, batches, own, features), bf),
            pltpu.VMEM((batches, 2, 4 * area, features), bf),
            pltpu.VMEM((batches, 2 * moved, features), bf),
            pltpu.VMEM((batches, 2 * moved, half_qkv), bf),
            pltpu.VMEM((batches, 2 * moved, inner), bf),
            pltpu.VMEM((batches, 2 * own, 2 * inner), bf),
            pltpu.VMEM((2, batches, own, features), bf),
            pltpu.VMEM((2, total, features), bf),
            pltpu.VMEM((2, total, half_up), bf),
            pltpu.VMEM((total, features), bf),
            pltpu.VMEM((total, features), bf),
            pltpu.VMEM((total, features), f32),
            pltpu.SemaphoreType.DMA((weight_sems,)),
            pltpu.SemaphoreType.DMA((weight_sems,)),
            pltpu.SemaphoreType.DMA((acts,)),
            pltpu.SemaphoreType.DMA((acts,)),
        ],
        compiler_params=pltpu.CompilerParams(
            collective_id=0, has_side_effects=True, vmem_limit_bytes=62 * 2**20
        ),
    )(
        offsets, levels, latents.reshape(total, features), mod_table.transpose(1, 0, 2), rel_bias, *shards
    )
    return found.reshape(latents.shape)


def solution(mesh):
    in_specs = (
        P("groups", None, "win", None),
        P("groups"),
        P("groups"),
        P(),
        P(),
        P("win", None),
        P("win", None),
        P("win", None),
        P("win", None),
    )
    out_specs = P("groups", None, "win", None)
    return jax.shard_map(local, mesh=mesh, in_specs=in_specs, out_specs=out_specs, check_vma=False)
```

```python
import functools

import jax
import jax.numpy as jnp
from jax import lax
from jax.experimental import pallas as pl
from jax.experimental.pallas import tpu as pltpu
from jax.sharding import PartitionSpec as P

HEADS = 6
HEAD_DIM = 128
WIN = 8
LEVELS = 32

MESH = pl.DeviceIdType.MESH
LINE = 4
LAT, STRIP, ATT, PART = 0, 3, 15, 18
PARTS = 6
UP_CHUNKS = 2
DOWN_SPLIT = (1, 2, 2, 1)
DOWN_CHUNKS = len(DOWN_SPLIT)


ORDER = (
    11, 12, 14, 0, 1, 10, 5, 2, 3, 7, 18, 20, 24, 90, 19, 9, 21, 32, 33, 4, 40, 34, 25, 13, 23,
    26, 8, 27, 15, 22, 6, 31, 41, 44, 79, 37, 28, 38, 42, 54, 16, 39, 116, 29, 52, 43, 17, 53,
    30, 35, 55, 45, 67, 36, 58, 48, 68, 66, 50, 65, 49, 46, 47, 103, 60, 56, 57, 59, 71, 69, 70,
    80, 78, 51, 61, 64, 74, 81, 77, 83, 88, 62, 91, 82, 72, 73, 89, 63, 75, 87, 92, 76, 84, 85,
    99, 102, 93, 94, 104, 96, 117, 98, 105, 101, 97, 95, 86, 106, 107, 111, 110, 112, 109, 115,
    100, 118, 124, 108, 119, 113, 120, 121, 114, 123, 122, 125,
)


def under(condition, act):
    if condition is None:
        act()
    else:
        pl.when(condition)(act)


def both(one, other):
    return other if one is None else one & other


class Chunk:
    count = 1 + 4 * LINE

    def __init__(self, full, depth, by_y, first, width, by_rows, base):
        self.full, self.depth, self.by_y = full, depth, by_y
        self.first, self.width, self.by_rows, self.base = first, width, by_rows, base

    def region(self, z, c, h=None, y=None):
        start, size = 0, self.depth
        first, width = self.first, self.width
        if h is not None and self.by_rows:
            size = self.depth // 2
            start = pl.multiple_of(h * size, 16)
        elif h is not None:
            width = self.width // 2
            first = pl.multiple_of(self.first + h * width, 128)
        rows, cols = pl.ds(start, size), pl.ds(first, width)
        if not self.by_y:
            return self.full.at[z, c, rows, cols]
        if y is None:
            return self.full.at[z, :, c, rows, cols]
        return self.full.at[z, y, c, rows, cols]

    def slot(self, kind, z):
        return self.base + 1 + kind * LINE + z


def flat(ref, cols):
    part = ref[(slice(None),) * (len(ref.shape) - 1) + (cols,)]
    return part.reshape(-1, part.shape[-1])


UPWARD, DOWNWARD, ACROSS, HAND = range(4)


class Gather:
    def __init__(self, send, recv):
        self.send, self.recv = send, recv
        me = lax.axis_index("win")
        self.c = lax.rem(me, 2)
        self.y = lax.rem(me // 2, 2)
        self.z = me // 4
        self.g = lax.axis_index("groups")
        self.x = lax.rem(self.g, 2)
        up, down = lax.rem(self.z + 1, LINE), lax.rem(self.z + LINE - 1, LINE)
        self.to_up = {"win": self.place(up, self.y, self.c)}
        self.to_down = {"win": self.place(down, self.y, self.c)}
        self.to_y = {"win": self.place(self.z, 1 - self.y, self.c)}
        self.to_core = {"win": self.place(self.z, self.y, 1 - self.c)}
        self.to_x = {"groups": self.g + 1 - 2 * self.x}
        far = lax.rem(self.z + 2 * self.c + LINE - 1, LINE)
        self.to_far = {"win": self.place(far, self.y, 1 - self.c)}
        self.started = []

    def place(self, z, y, c):
        return (z * 2 + y) * 2 + c

    def neighbours(self):
        return [self.to_up, self.to_down, self.to_y, self.to_core, self.to_x, self.to_far]

    def copy(self, slot, src, dst, to):
        return pltpu.make_async_remote_copy(
            src_ref=src,
            dst_ref=dst,
            send_sem=self.send.at[slot],
            recv_sem=self.recv.at[slot],
            device_id=to,
            device_id_type=MESH,
        )

    def put(self, condition, make):
        under(condition, lambda: make().start())
        self.started.append((condition, make))

    def pass_on(self, condition, slot, part, to):
        self.put(condition, lambda: self.copy(slot, part(), part(), to))

    def arrive(self, condition, slot, part):
        under(condition, lambda: self.copy(slot, part(), part(), self.to_core).wait_recv())

    def y_send(self, t, source):
        part = lambda: t.region(self.z, self.c, self.x, self.y)
        self.put(None, lambda: self.copy(t.base, source(), part(), self.to_y))

    def own(self, t):
        part = lambda: t.region(self.z, self.c, self.x)
        self.pass_on(self.z >= 1, t.slot(DOWNWARD, self.z), part, self.to_down)
        self.pass_on(self.z + 1 < LINE, t.slot(UPWARD, self.z), part, self.to_up)

    def y_come(self, t):
        part = lambda: t.region(self.z, self.c, self.x, 1 - self.y)
        self.arrive(None, t.base, part)
        self.own(t)
        self.pass_on(None, t.slot(ACROSS, self.z), part, self.to_x)

    def sources(self, d):
        if d == 0:
            return ((None, self.z),)
        return ((self.z >= d, self.z - d), (self.z + d < LINE, self.z + d))

    def z_come(self, t, d):
        ways = ((UPWARD, self.z + 1 < LINE, self.to_up), (DOWNWARD, self.z >= 1, self.to_down))
        for (there, z), (way, more, to) in zip(self.sources(d), ways):
            part = lambda z=z: t.region(z, self.c, self.x)
            self.arrive(there, t.slot(way, z), part)
            if d < LINE - 1:
                self.pass_on(there & more, t.slot(way, z), part, to)
            self.pass_on(there, t.slot(ACROSS, z), part, self.to_x)

    def x_come(self, t, d):
        for there, z in self.sources(d):
            if d > 0:
                self.arrive(there, t.slot(ACROSS, z), lambda z=z: t.region(z, self.c, 1 - self.x))
            elif t.by_y:
                part = lambda: t.region(self.z, self.c, 1 - self.x, 1 - self.y)
                self.arrive(None, t.slot(ACROSS, self.z), part)
            self.pass_on(there, t.slot(HAND, z), lambda z=z: t.region(z, self.c), self.to_core)

    def handed(self, t):
        for z in range(LINE):
            self.arrive(None, t.slot(HAND, z), lambda z=z: t.region(z, 1 - self.c))

    def drain(self):
        for condition, make in self.started:
            under(condition, lambda make=make: make().wait_send())


def meet(neighbours):
    barrier = pltpu.get_barrier_semaphore()
    for to in neighbours:
        pl.semaphore_signal(barrier, inc=1, device_id=to, device_id_type=MESH)
    pl.semaphore_wait(barrier, len(neighbours))


def norm_rows(values_in):
    centre = values_in - jnp.mean(values_in, axis=-1, keepdims=True)
    spread = jnp.mean(centre * centre, axis=-1, keepdims=True)
    return centre * lax.rsqrt(spread + 1e-06)


def passed_along(shard, axis, by):
    length = lax.axis_size(axis)
    return lax.ppermute(shard, axis, [(i, (i + by) % length) for i in range(length)])


def cut(widened, starts, columns):
    return jnp.stack(
        [
            lax.dynamic_slice_in_dim(widened[m], starts[m], columns, 1)
            for m in range(widened.shape[0])
        ]
    )


def restore_grid(region, arrived, offsets, columns):
    return cut(jnp.concatenate([region, arrived], axis=2), offsets, columns)


def plain(latents, offsets, levels, mod_table, rel_bias, w_qkv, w_out, w_up, w_down):
    batches, lat_rows, columns, features = latents.shape
    inner = HEADS * HEAD_DIM
    per_dev = columns // WIN
    selector = (levels[:, None] == jnp.arange(LEVELS, dtype=jnp.int32)[None, :]).astype(
        jnp.bfloat16
    )
    modulation = jnp.dot(
        selector, mod_table.reshape(LEVELS, 6 * features), preferred_element_type=jnp.float32
    )
    modulation = modulation.reshape(batches, 6, 1, 1, features)
    stream = latents.astype(jnp.float32)
    normed = (norm_rows(stream) * (1.0 + modulation[:, 0]) + modulation[:, 1]).astype(jnp.bfloat16)
    arrived = passed_along(normed[:, :, columns - WIN :, :], "win", 1)
    widened = jnp.concatenate([arrived, normed], axis=2)
    rolled = cut(widened, WIN - offsets, columns)
    full_qkv = lax.all_gather(w_qkv, "win", axis=0, tiled=True)
    windows = rolled.reshape(batches, lat_rows, per_dev, WIN, features).transpose(0, 2, 1, 3, 4)
    windows = windows.reshape(-1, lat_rows * WIN, features)
    number = windows.shape[0]
    triple = jnp.dot(windows.reshape(-1, features), full_qkv, preferred_element_type=jnp.float32)
    triple = triple.astype(jnp.bfloat16).reshape(number, lat_rows * WIN, 3, HEADS, HEAD_DIM)
    scores = jnp.einsum(
        "wqhe,wkhe->whqk", triple[:, :, 0], triple[:, :, 1], preferred_element_type=jnp.float32
    )
    scores = scores * (1.0 / HEAD_DIM**0.5) + rel_bias[None]
    probs = jax.nn.softmax(scores, axis=-1).astype(jnp.bfloat16)
    attended = jnp.einsum(
        "whqk,wkhe->wqhe", probs, triple[:, :, 2], preferred_element_type=jnp.float32
    ).astype(jnp.bfloat16)
    attended = attended.reshape(batches, per_dev, lat_rows, WIN, inner).transpose(0, 2, 1, 3, 4)
    attended = attended.reshape(batches, lat_rows, columns, inner)
    full_out = lax.all_gather(w_out, "win", axis=0, tiled=True)
    returned = passed_along(attended[:, :, :WIN, :], "win", -1)
    restored = restore_grid(attended, returned, offsets, columns)
    projected = jnp.dot(restored.reshape(-1, inner), full_out, preferred_element_type=jnp.float32)
    projected = projected.reshape(batches, lat_rows, columns, features)
    middle = (stream + modulation[:, 2] * projected).astype(jnp.bfloat16)
    second = (
        norm_rows(middle.astype(jnp.float32)) * (1.0 + modulation[:, 3]) + modulation[:, 4]
    ).astype(jnp.bfloat16)
    full_up = lax.all_gather(w_up, "win", axis=0, tiled=True)
    hidden = jnp.dot(second.reshape(-1, features), full_up, preferred_element_type=jnp.float32)
    hidden = jax.nn.gelu(hidden, approximate=False).astype(jnp.bfloat16)
    full_down = lax.all_gather(w_down, "win", axis=0, tiled=True)
    lowered = jnp.dot(hidden, full_down, preferred_element_type=jnp.float32).reshape(
        batches, lat_rows, columns, features
    )
    return (middle.astype(jnp.float32) + modulation[:, 5] * lowered).astype(jnp.bfloat16)


def repeat(count, act):
    lax.fori_loop(0, count, lambda i, _: (act(i), 0)[1], 0)


def chunks_of(shapes, fulls):
    (q, o, u, d), base, made = shapes, 0, []

    def take(full, shape, split, by_y, by_rows):
        nonlocal base
        unit, first = full[1] // sum(split), 0
        for part in split:
            ref = None if fulls is None else fulls[full[0]]
            made.append(Chunk(ref, shape[0], by_y, first, part * unit, by_rows, base))
            base += Chunk.count
            first += part * unit

    take((0, q[1] // 2), q, (1,), True, True)
    take((1, o[1]), o, (1,), True, False)
    take((2, u[1] // 2), u, (1,) * UP_CHUNKS, True, True)
    take((3, d[1]), d, DOWN_SPLIT, False, True)
    return made, base


def kernel(
    batches, area, offsets_ref, levels_ref, lat_ref, table_ref, bias_ref, s0, s1, s2, s3, out_ref,
    f0, f1, f2, f3, a0, a2, mod, bias, scores, probs, gather_in, gather_out, lat, wide, wins, triple, heads, att, middle,
    second, hidden, part_out, part_in, part_own, send, recv, act_send, act_recv, near,
):
    features = lat_ref.shape[1]
    own = lat_ref.shape[0] // batches
    moved = gather_in.shape[1]
    inner = f0.shape[-1] // 3
    pair_heads = inner // HEAD_DIM
    bf, f32 = jnp.bfloat16, jnp.float32
    chunks, _ = chunks_of((s0.shape, s1.shape, s2.shape, s3.shape), (f0, f1, f2, f3))
    cq, co, cu, cd = chunks[0], chunks[1], chunks[2 : 2 + UP_CHUNKS], chunks[2 + UP_CHUNKS :]
    net = Gather(send, recv)
    x, y, z, c = net.x, net.y, net.z, net.c
    other = 1 - y

    def activation(send_at, recv_at, src, dst, to):
        def make():
            return pltpu.make_async_remote_copy(
                src_ref=src(),
                dst_ref=dst(),
                send_sem=act_send.at[send_at],
                recv_sem=act_recv.at[recv_at],
                device_id=to,
                device_id_type=MESH,
            )

        net.put(None, make)

    def landed(recv_at, dst):
        pltpu.make_async_remote_copy(
            src_ref=dst,
            dst_ref=dst,
            send_sem=act_send.at[recv_at],
            recv_sem=act_recv.at[recv_at],
            device_id=net.to_core,
            device_id_type=MESH,
        ).wait_recv()

    def lay_qkv():
        for which in range(3):
            for k in range(2):
                first = (which * 2 + k) * inner
                a0[k, :, which * inner : (which + 1) * inner] = s0[:, first : first + inner]
        f0[z, y, c] = a0[y]

    def lay_out():
        straight[0].wait()

    block = s3.shape[0] * 2

    def lay_up():
        for at in range(LINE):
            for k in range(2):
                first = (at * 2 + k) * block
                a2[k, :, at * block : (at + 1) * block] = s2[:, first : first + block]
        f2[z, y, c] = a2[y]

    def lay_down():
        straight[1].wait()

    def half_rows(ref, t):
        size = t.depth // 2
        rows = pl.ds(pl.multiple_of(x * size, 16), size)
        return lambda: ref.at[other, rows, pl.ds(t.first, t.width)]

    def send_lat(m):
        activation(
            LAT + m, LAT + m, lambda: lat_ref.at[pl.ds(m * own, own)], lambda: lat.at[y, m], net.to_y
        )

    def modulate():
        shape = (8, table_ref.shape[1])
        row = lax.broadcasted_iota(jnp.int32, shape, 0)
        level = lax.broadcasted_iota(jnp.int32, shape, 1)
        hit = (row == 0) & (level == levels_ref[0])
        for m in range(1, batches):
            hit = hit | ((row == m) & (level == levels_ref[m]))
        pick = jnp.where(hit, 1.0, 0.0).astype(bf)
        for k in range(table_ref.shape[0]):
            found = jnp.dot(pick, table_ref[k], preferred_element_type=f32)
            for m in range(batches):
                mod[m, k : k + 1, :] = found[m : m + 1, :]

    def make_moves():
        i = lax.broadcasted_iota(jnp.int32, (moved, wide.shape[2]), 0)
        j = lax.broadcasted_iota(jnp.int32, (moved, wide.shape[2]), 1)
        to_row, to_at = (i >> 3) & 7, ((i >> 6) << 3) + (i & 7)
        from_row, from_at = (j >> 3) & 7, ((j >> 6) << 3) + (j & 7)
        same = to_row == from_row
        k = lax.broadcasted_iota(jnp.int32, (own, moved), 0)
        n = lax.broadcasted_iota(jnp.int32, (own, moved), 1)
        back = (k >> 4) == ((n >> 3) & 7)
        back_at, rolled_at = k & 15, ((n >> 6) << 3) + (n & 7)
        for m in range(batches):
            by = offsets_ref[m]
            hit = same & (to_at + WIN - by == from_at)
            gather_in[m] = jnp.where(hit, 1.0, 0.0).astype(bf)
            hit = back & (back_at + by == rolled_at)
            gather_out[m] = jnp.where(hit, 1.0, 0.0).astype(bf)

    def copy_own():
        for m in range(batches):
            lat[y, m] = lat_ref[m * own : (m + 1) * own, :]

    def norm_tile(m, slot):
        def step(i):
            rows = lat[slot, m, i * 32 : (i + 1) * 32, :].astype(f32)
            value = norm_rows(rows) * (1.0 + mod[m, 0:1, :]) + mod[m, 1:2, :]
            value = value.reshape(2, 2, WIN, features)
            for half in range(2):
                start = (half + 1) * area + i * 16
                wide[m, slot, start : start + 16, :] = value[:, half].reshape(16, features).astype(bf)

        for i in range(own // 32):
            step(i)

    def strip(m, slot, at):
        return wide.at[m, slot, pl.ds(at * area, area)]

    def send_strips(m, slot):
        base = STRIP + m * 4
        low_slot = (1 - c) * (1 - slot) + c * slot
        low_z = lax.rem(z + LINE - (1 - c) * (1 - slot), LINE)
        activation(
            base + slot * 2, base + low_slot * 2 + 1,
            lambda: strip(m, slot, 1), lambda: strip(m, low_slot, 3),
            {"win": net.place(low_z, y, 1 - c)},
        )
        high_slot = (1 - c) * slot + c * (1 - slot)
        high_z = lax.rem(z + c * slot, LINE)
        activation(
            base + slot * 2 + 1, base + high_slot * 2,
            lambda: strip(m, slot, 2), lambda: strip(m, high_slot, 0),
            {"win": net.place(high_z, y, 1 - c)},
        )

    def norm_own(m):
        norm_tile(m, y)
        send_strips(m, y)

    def norm_other(m):
        landed(LAT + m, lat.at[other, m])
        norm_tile(m, other)
        send_strips(m, other)

    def windows(m):
        for slot in range(2):
            landed(STRIP + m * 4 + slot * 2, strip(m, slot, 0))
            landed(STRIP + m * 4 + slot * 2 + 1, strip(m, slot, 3))
        for slot in range(2):
            wins[m, slot * moved : (slot + 1) * moved, :] = jnp.dot(
                gather_in[m], wide[m, slot], preferred_element_type=f32
            ).astype(bf)

        def project(cols):
            triple[m, :, cols] = jnp.dot(
                wins[m], flat(f0, cols), preferred_element_type=f32
            ).astype(bf)

        whole = f0.shape[-1] // width
        repeat(whole, lambda i: project(columns(i)))
        project(slice(whole * width, f0.shape[-1]))

    def make_bias():
        for head in range(pair_heads):
            one = bias_ref[y * pair_heads + head]
            rest = jnp.full(one.shape, -1e30, f32)
            bias[head, :area, :] = jnp.concatenate([one, rest], axis=1)
            bias[head, area:, :] = jnp.concatenate([rest, one], axis=1)

    def attend(m):
        pair = 2 * area
        spans = [
            (w * pair, head * HEAD_DIM, head)
            for w in range(moved // area)
            for head in range(pair_heads)
        ]

        def of(which, row, first):
            first = which * inner + first
            return triple[m, row : row + pair, first : first + HEAD_DIM]

        for i, (row, first, head) in enumerate(spans):
            found = lax.dot_general(
                of(0, row, first), of(1, row, first), (((1,), (1,)), ((), ())),
                preferred_element_type=f32,
            )
            scores[i * pair : (i + 1) * pair, :] = found * (1.0 / HEAD_DIM**0.5) + bias[head]
        group = pair_heads * pair
        for i in range(moved // area):
            rows = slice(i * group, (i + 1) * group)
            powers = scores[rows, :]
            powers = jnp.exp(powers - jnp.max(powers, axis=-1, keepdims=True))
            inverse = 1.0 / jnp.sum(powers, axis=-1, keepdims=True)
            probs[rows, :] = (powers * inverse).astype(bf)
        for i, (row, first, head) in enumerate(spans):
            heads[m, row : row + pair, first : first + HEAD_DIM] = jnp.dot(
                probs[i * pair : (i + 1) * pair, :], of(2, row, first), preferred_element_type=f32
            ).astype(bf)

        mine = pl.ds(pl.multiple_of(y * inner, 128), inner)
        for slot in range(2):
            att[m, pl.ds(slot * own, own), mine] = jnp.dot(
                gather_out[m], heads[m, slot * moved : (slot + 1) * moved, :],
                preferred_element_type=f32,
            ).astype(bf)
        activation(
            ATT + m, ATT + m, lambda: att.at[m, :, mine], lambda: att.at[m, :, mine], net.to_y
        )

    width = 256

    def columns(i):
        return pl.ds(pl.multiple_of(i * width, width), width)

    def settle(m):
        theirs = pl.ds(pl.multiple_of(other * inner, 128), inner)
        landed(ATT + m, att.at[m, :, theirs])

        def piece(i):
            cols = columns(i)
            found = jnp.dot(att[m], flat(f1, cols), preferred_element_type=f32)
            for slot in range(2):
                change = mod[m, 2:3, cols] * found[slot * own : (slot + 1) * own]
                middle[slot, m, :, cols] = (lat[slot, m, :, cols].astype(f32) + change).astype(bf)

        repeat(features // width, piece)
        for slot in range(2):
            for i in range(own // 32):
                rows = middle[slot, m, i * 32 : (i + 1) * 32, :].astype(f32)
                value = norm_rows(rows) * (1.0 + mod[m, 3:4, :]) + mod[m, 4:5, :]
                start = m * own + i * 32
                second[slot, start : start + 32, :] = value.astype(bf)

    def lift(first, count):
        def piece(i):
            cols = columns(first + i)
            for slot in range(2):
                found = jnp.dot(second[slot], flat(f2, cols), preferred_element_type=f32)
                found = 0.5 * found * (1.0 + lax.erf(found * (0.5**0.5)))
                hidden[slot, :, cols] = found.astype(bf)

        repeat(count, piece)

    part = features // PARTS

    def lower(j):
        cols = slice(j * part, (j + 1) * part)
        part_out[:, cols] = jnp.dot(
            hidden[other], flat(f3, cols), preferred_element_type=f32
        ).astype(bf)
        activation(
            PART + j, PART + j, lambda: part_out.at[:, cols], lambda: part_in.at[:, cols], net.to_y
        )

    def lower_own(j):
        cols = slice(j * part, (j + 1) * part)
        part_own[:, cols] = jnp.dot(hidden[y], flat(f3, cols), preferred_element_type=f32)

    def finish(j):
        cols = slice(j * part, (j + 1) * part)
        landed(PART + j, part_in.at[:, cols])
        for m in range(batches):
            rows = slice(m * own, (m + 1) * own)
            change = part_own[rows, cols] + part_in[rows, cols].astype(f32)
            out_ref[rows, cols] = (
                middle[y, m, :, cols].astype(f32) + mod[m, 5:6, cols] * change
            ).astype(bf)

    steps = []

    def at(time, act, *args):
        steps.append((time, len(steps), functools.partial(act, *args)))

    def across(t, when):
        for d in range(LINE):
            at(when, net.x_come, t, d)

    at(0, lay_qkv)
    at(0, net.y_send, cq, half_rows(a0, cq))
    at(0.5, lay_out)
    at(0.5, net.y_send, co, lambda: co.region(z, c, x, y))
    at(0.5, send_lat, 0)
    at(0.6, lay_up)
    at(0.6, net.y_send, cu[0], half_rows(a2, cu[0]))
    at(0.7, send_lat, 1)
    at(0.7, net.y_send, cu[1], half_rows(a2, cu[1]))
    at(0.8, send_lat, 2)
    at(0.8, lay_down)
    at(0.9, copy_own)
    at(1, modulate)
    for m in range(batches):
        at(1 + 0.1 * m, norm_own, m)
    at(3.8, make_moves)
    at(3.9, make_bias)
    hops = ((7, 13, 19), (25, 29, 33), (37, 41, 45), (49, 53, 57)) + (
        (60, 62, 64), (65, 66, 68), (72, 74, 77), (80, 82, 85)
    )
    at(4, net.y_come, cq)
    for i, t in enumerate(chunks):
        for d, when in enumerate(hops[i]):
            at(when, net.z_come, t, d + 1)
        if i == 0:
            across(t, 22.5)
        elif i + 1 < len(chunks):
            across(t, hops[i + 1][0] + 0.05)
        else:
            across(t, hops[i][2] + 0.1)
        if i + 1 < len(chunks):
            at(hops[i][0] - 0.1, net.y_come if chunks[i + 1].by_y else net.own, chunks[i + 1])
    for m, when in enumerate((15, 26.5, 38)):
        at(when, norm_other, m)
    at(22.9, net.handed, cq)
    for m, when in enumerate((23, 31, 43)):
        at(when, windows, m)
        at(when + 0.1, attend, m)
    at(41.9, net.handed, co)
    for m, when in enumerate((42, 46, 56)):
        at(when, settle, m)
    each = f2.shape[-1] // width // UP_CHUNKS
    for i, (t, when) in enumerate(zip(cu, (57, 63.5))):
        at(when, net.handed, t)
        for k in range(each):
            at(when + 0.5 * k, lift, i * each + k, 1)
    done = 0
    for t, when in zip(cd, (66.5, 73, 81, 86)):
        at(when, net.handed, t)
        for k in range(t.width // part):
            at(when + 0.1, lower, done)
            at(when + 0.2, lower_own, done)
            done += 1
    for j, when in enumerate((74, 82, 82.5, 87, 88, 89)):
        at(when, finish, j)

    straight = [
        pltpu.make_async_copy(s1, f1.at[z, y, c], near.at[0]),
        pltpu.make_async_copy(s3, f3.at[z, c], near.at[1]),
    ]
    for made in straight:
        made.start()
    meet(net.neighbours())
    listed = sorted(steps, key=lambda step: step[:2])
    for i in ORDER:
        listed[i][2]()
    net.drain()


def local(latents, offsets, levels, mod_table, rel_bias, w_qkv, w_out, w_up, w_down):
    count = lax.axis_size("win")
    batches, lat_rows, columns, features = latents.shape
    fits = count == 4 * LINE and lax.axis_size("groups") % 2 == 0 and columns == 2 * WIN
    if not (fits and lat_rows == WIN and batches == 3):
        return plain(
            latents, offsets, levels, mod_table, rel_bias, w_qkv, w_out, w_up, w_down
        )
    area = lat_rows * WIN
    own, moved = lat_rows * columns, 3 * area
    shards = (w_qkv, w_out, w_up, w_down)
    total = batches * own
    half_qkv, half_up = w_qkv.shape[1] // 2, w_up.shape[1] // 2
    inner = half_qkv // 3
    _, weight_sems = chunks_of([s.shape for s in shards], None)
    acts = PART + PARTS
    vmem = pl.BlockSpec(memory_space=pltpu.VMEM)
    smem = pl.BlockSpec(memory_space=pltpu.SMEM)
    hbm = pl.BlockSpec(memory_space=pl.ANY)
    bf, f32 = jnp.bfloat16, jnp.float32
    found = pl.pallas_call(
        functools.partial(kernel, batches, area),
        out_shape=jax.ShapeDtypeStruct((total, features), bf),
        in_specs=[smem] * 2 + [vmem] * 4 + [hbm, vmem, hbm],
        out_specs=vmem,
        scratch_shapes=[
            pltpu.VMEM((LINE, 2, 2, w_qkv.shape[0], half_qkv), bf),
            pltpu.VMEM((LINE, 2, 2, w_out.shape[0], features), bf),
            pltpu.VMEM((LINE, 2, 2, w_up.shape[0], half_up), bf),
            pltpu.VMEM((LINE, 2, w_down.shape[0], features), bf),
            pltpu.VMEM((2, w_qkv.shape[0], half_qkv), bf),
            pltpu.VMEM((2, w_up.shape[0], half_up), bf),
            pltpu.VMEM((batches, 6, features), f32),
            pltpu.VMEM((HEADS // 2, 2 * area, 2 * area), f32),
            pltpu.VMEM((HEADS // 2 * 6 * area, 2 * area), f32),
            pltpu.VMEM((HEADS // 2 * 6 * area, 2 * area), bf),
            pltpu.VMEM((batches, moved, 4 * area), bf),
            pltpu.VMEM((batches, own, moved), bf),
            pltpu.VMEM((2, batches, own, features), bf),
            pltpu.VMEM((batches, 2, 4 * area, features), bf),
            pltpu.VMEM((batches, 2 * moved, features), bf),
            pltpu.VMEM((batches, 2 * moved, half_qkv), bf),
            pltpu.VMEM((batches, 2 * moved, inner), bf),
            pltpu.VMEM((batches, 2 * own, 2 * inner), bf),
            pltpu.VMEM((2, batches, own, features), bf),
            pltpu.VMEM((2, total, features), bf),
            pltpu.VMEM((2, total, half_up), bf),
            pltpu.VMEM((total, features), bf),
            pltpu.VMEM((total, features), bf),
            pltpu.VMEM((total, features), f32),
            pltpu.SemaphoreType.DMA((weight_sems,)),
            pltpu.SemaphoreType.DMA((weight_sems,)),
            pltpu.SemaphoreType.DMA((acts,)),
            pltpu.SemaphoreType.DMA((acts,)),
            pltpu.SemaphoreType.DMA((2,)),
        ],
        compiler_params=pltpu.CompilerParams(
            collective_id=0, has_side_effects=True, vmem_limit_bytes=62 * 2**20
        ),
    )(
        offsets, levels, latents.reshape(total, features), mod_table.transpose(1, 0, 2), rel_bias, *shards
    )
    return found.reshape(latents.shape)


def solution(mesh):
    in_specs = (
        P("groups", None, "win", None),
        P("groups"),
        P("groups"),
        P(),
        P(),
        P("win", None),
        P("win", None),
        P("win", None),
        P("win", None),
    )
    out_specs = P("groups", None, "win", None)
    return jax.shard_map(local, mesh=mesh, in_specs=in_specs, out_specs=out_specs, check_vma=False)
```
